32 devices in a mesh: dp: 4 (over x, core), ctx: 8 (over z, y).
Axes of the slice: x: 2, y: 2, z: 4, core: 2. Of those that a mesh axis runs over, the one named last changes fastest.
Arguments:
- queries: bfloat16 [4, 4096, 512], P('dp', 'ctx'), may hold values from -12 to 12
- keys: bfloat16 [4, 4096, 128], P('dp', 'ctx'), may hold values from -12 to 12
- values: bfloat16 [4, 4096, 128], P('dp', 'ctx'), may hold values from -6 to 6
- doc_lengths: int32 [4, 8], P('dp'), may hold values from 1 to 2048, as said below
- owner: int32 [4, 64], P('dp'), may hold values from 0 to 7, as said below
- out_weight: bfloat16 [512, 4096], replicated, may hold values from -0.25 to 0.25
- out_grad: bfloat16 [4, 4096, 4096], P('dp', 'ctx'), may hold values from -6 to 6
Outputs:
- attn_out: bfloat16 [4, 4096, 512], P('dp', 'ctx')
- q_grad: bfloat16 [4, 4096, 512], P('dp', 'ctx')
- k_grad: bfloat16 [4, 4096, 128], P('dp', 'ctx')
- v_grad: bfloat16 [4, 4096, 128], P('dp', 'ctx')
- wo_grad: float32 [512, 4096], P(None, ('dp', 'ctx'))
- owner_lse: float32 [4, 8, 512, 4], P('dp', 'ctx')
The draws below stay inside these ranges and needn't reach their ends.
Inputs may be any that keep to these rules, and one draw needn't show every extreme that they name: `doc_lengths`: the 8 lengths of a sequence sum to 4096; the largest is exactly 2048. owner[s, b] names the device of ctx that handles block b of 64 tokens of sequence s; the blocks that lie on one device go to distinct devices, one to each.
All inputs are finite; a program needn't handle non-finite values.
Results may differ from the reference program's by a relative error of at most 0.014.
Values may be sent and summed in bfloat16 or wider, within the bound.
No kernel may reach another device: no remote copies, remote signals or barrier semaphores. Data moves between devices by JAX's collectives and lax.ppermute only.
A program may use at most 256 MiB of HBM per device.

```python
import math
import jax
import jax.numpy as jnp
from jax import lax

D = 4096
HEAD = 128
GROUP = 4
KV_HEADS = 1
WIN = 4096
NDOC = 8
TOK_DEV = 512
HQ = 4
QW = 512
KW = 128
SEQS = 4
SEQ = 4096
BLK = 64
NB = 64
MOST = 2048
N_CTX = 8


def lengths_all(key):
    base = jax.random.fold_in(key, 5)
    rest = SEQ - MOST

    def one_sequence(subkey):
        cut_key, slot_key = jax.random.split(subkey)
        cuts = jnp.sort(jax.random.permutation(cut_key, rest - 1)[:NDOC - 2] + 1).astype(jnp.int32)
        edges = jnp.concatenate([jnp.zeros((1,), jnp.int32), cuts, jnp.full((1,), rest, jnp.int32)])
        others = edges[1:] - edges[:-1]
        chosen = jax.random.randint(slot_key, (), 0, NDOC)
        ladder = jnp.arange(NDOC, dtype=jnp.int32)
        lower = others[jnp.clip(ladder, 0, NDOC - 2)]
        upper = others[jnp.clip(ladder - 1, 0, NDOC - 2)]
        return jnp.where(ladder < chosen, lower, jnp.where(ladder == chosen, MOST, upper)).astype(jnp.int32)
    return jax.vmap(one_sequence)(jax.random.split(base, SEQS))


def draw_doc_lengths(key, part):
    return lengths_all(key)


def draw_owner(key, part):
    lengths = lengths_all(key)
    mixers = jax.random.split(jax.random.fold_in(key, 9), SEQS)
    devices = SEQ // TOK_DEV

    def one_sequence(lens, subkey):
        positions = jnp.arange(SEQ, dtype=jnp.int32)
        ends = jnp.cumsum(lens).astype(jnp.int32)
        starts = ends - lens
        inside = (positions[:, None] >= starts[None, :]) & (positions[:, None] < ends[None, :])
        start = jnp.sum(jnp.where(inside, starts[None, :], 0), axis=1)
        cost = jnp.minimum(positions - start + 1, WIN)
        block_cost = cost.reshape(devices, devices, BLK).sum(axis=2)
        ladder = jnp.arange(devices, dtype=jnp.int32)
        score = block_cost * devices + ladder[None, :]
        rank = jnp.argsort(jnp.argsort(score, axis=1), axis=1).astype(jnp.int32)
        shuffle = jax.random.permutation(subkey, devices).astype(jnp.int32)
        return shuffle[(rank + ladder[:, None]) % devices].reshape(-1).astype(jnp.int32)
    return jax.vmap(one_sequence)(lengths, mixers)


def draw_queries(key, part):
    noise_key = jax.random.fold_in(key, 1)
    return jnp.clip(jax.random.normal(noise_key, (SEQS, SEQ, QW)), -6.0, 6.0).astype(jnp.bfloat16)


def draw_keys(key, part):
    noise_key = jax.random.fold_in(key, 2)
    return jnp.clip(jax.random.normal(noise_key, (SEQS, SEQ, KW)), -6.0, 6.0).astype(jnp.bfloat16)


def raised(result, rng, source, target, parts, factor):
    owner, partner = [(jnp.arange(result.shape[position]) // (result.shape[position] // parts)).reshape([-1 if axis == position else 1 for axis in range(result.ndim)]) for position in (source, target)]
    chosen = jax.random.permutation(rng, parts)[partner]
    strong = (owner == chosen) | (owner == (partner + parts // 2) % parts)
    return jnp.where(strong, factor * result, result)


def shard_levels(own_key, extent, cuts, low, high):
    factor_of, own = 1.0, jax.random.fold_in(own_key, 6)
    for axis_at, parts in cuts:
        steps = jnp.exp(jax.random.uniform(jax.random.fold_in(own, axis_at), (parts,), jnp.float32, low / len(cuts), high / len(cuts)))
        factor_of = factor_of * jnp.repeat(steps, extent[axis_at] // parts).reshape([-1 if axis == axis_at else 1 for axis in range(len(extent))])
    return factor_of


def scatter_about(rng, shape, scale, bound, pieces=(), kind=jnp.bfloat16):
    entries = jax.random.normal(rng, shape, jnp.float32) * scale
    if len(pieces) > 0:
        entries = shard_levels(rng, shape, pieces, -0.22, 0.18) * entries
    return jnp.clip(entries, min=-bound, max=bound).astype(kind)


def noise_with(rng, dims, spread, limit, shards, heavy, held_as=jnp.bfloat16):
    result = spread * jax.random.normal(rng, dims, jnp.float32)
    if shards:
        result = result * shard_levels(rng, dims, shards, -0.22, 0.18)
    return jnp.clip(raised(result, jax.random.fold_in(rng, 3), *heavy), -limit, limit).astype(held_as)


def setup_inputs(seed: int = 0) -> dict:
    streams_of = jax.random.split(jax.random.key(seed), 8)
    return {
        "queries": draw_queries(jax.random.fold_in(streams_of[7], 71), 0),
        "keys": draw_keys(jax.random.fold_in(streams_of[7], 71), 0),
        "values": scatter_about(streams_of[2], (SEQS, SEQ, KW), 1.0, 6.0, ((0, 4), (1, 8))),
        "doc_lengths": draw_doc_lengths(jax.random.fold_in(streams_of[7], 71), 0),
        "owner": draw_owner(jax.random.fold_in(streams_of[7], 71), 0),
        "out_weight": scatter_about(streams_of[5], (QW, D), QW ** -0.5, 0.25),
        "out_grad": noise_with(streams_of[6], (SEQS, SEQ, D), 1.0, 6.0, ((0, 4), (1, 8)), (1, 2, 8, 2.0)),
    }


NEG = -1e+30

def rotate(values_in, offsets, sign):
    half = values_in.shape[-1] // 2
    ladder = jnp.arange(half, dtype=jnp.int32).astype(jnp.float32)
    freq = 10000.0 ** (-2.0 * ladder / values_in.shape[-1])
    angle = offsets.astype(jnp.float32)[:, None] * freq[None, :]
    cosine = jnp.cos(angle)[:, None, :]
    sine = sign * jnp.sin(angle)[:, None, :]
    first = values_in[..., :half]
    second = values_in[..., half:]
    return jnp.concatenate([first * cosine - second * sine, second * cosine + first * sine], axis=-1)

def doc_start(lengths, positions):
    ends = jnp.cumsum(lengths).astype(jnp.int32)
    starts = ends - lengths.astype(jnp.int32)
    inside = (positions[:, None] >= starts[None, :]) & (positions[:, None] < ends[None, :])
    return lax.optimization_barrier(jnp.sum(jnp.where(inside, starts[None, :], 0), axis=1)).astype(jnp.int32)

def reference(queries, keys, values, doc_lengths, owner, out_weight, out_grad):
    scale = 1.0 / math.sqrt(HEAD)
    span = WIN + BLK
    counter = jnp.arange(N_CTX, dtype=jnp.int32)

    def one_sequence(items):
        seq_q, seq_k, seq_v, lengths, owners, seq_dy = items
        positions = jnp.arange(SEQ, dtype=jnp.int32)
        starts = doc_start(lengths, positions)
        rel = positions - starts
        q_rot = rotate(seq_q.astype(jnp.float32).reshape(SEQ, HQ, HEAD), rel, 1.0).astype(jnp.bfloat16)
        k_rot = rotate(seq_k.astype(jnp.float32).reshape(SEQ, KV_HEADS, HEAD), rel, 1.0).astype(jnp.bfloat16)
        d_out = lax.dot_general(seq_dy, out_weight, (((1,), (1,)), ((), ())), preferred_element_type=jnp.float32).astype(jnp.bfloat16)
        key_pad = jnp.concatenate([jnp.zeros((WIN, KV_HEADS, HEAD), jnp.bfloat16), k_rot], axis=0)
        value_pad = jnp.concatenate([jnp.zeros((WIN, KV_HEADS, HEAD), jnp.bfloat16), seq_v.reshape(SEQ, KV_HEADS, HEAD)], axis=0)
        grid = owners.reshape(N_CTX, N_CTX)

        def one_block(first):
            rows = first + jnp.arange(BLK, dtype=jnp.int32)
            row_start = lax.dynamic_slice_in_dim(starts, first, BLK, 0)
            query_f = lax.dynamic_slice_in_dim(q_rot, first, BLK, 0).astype(jnp.float32).reshape(BLK, KV_HEADS, GROUP, HEAD)
            grad_f = lax.dynamic_slice_in_dim(d_out, first, BLK, 0).astype(jnp.float32).reshape(BLK, KV_HEADS, GROUP, HEAD)
            key_f = lax.dynamic_slice_in_dim(key_pad, first, span, 0).astype(jnp.float32)
            value_f = lax.dynamic_slice_in_dim(value_pad, first, span, 0).astype(jnp.float32)
            key_pos = first - WIN + jnp.arange(span, dtype=jnp.int32)
            allowed = (key_pos[None, :] >= row_start[:, None]) & (key_pos[None, :] <= rows[:, None]) & (key_pos[None, :] > rows[:, None] - WIN)
            scores = jnp.einsum('qhed,khd->heqk', query_f, key_f) * scale
            scores = jnp.where(allowed, scores, NEG)
            top = lax.optimization_barrier(jnp.max(scores, axis=-1, keepdims=True))
            total = lax.optimization_barrier(jnp.sum(jnp.where(allowed, jnp.exp(scores - top), 0.0), axis=-1, keepdims=True))
            lse = top + jnp.log(total)
            prob = jnp.where(allowed, jnp.exp(scores - lse), 0.0)
            prob_r = lax.optimization_barrier(prob.astype(jnp.bfloat16)).astype(jnp.float32)
            attn = jnp.einsum('heqk,khd->qhed', prob_r, value_f).astype(jnp.bfloat16)
            attn_f = attn.astype(jnp.float32)
            delta = lax.optimization_barrier(jnp.sum(grad_f * attn_f, axis=-1)).transpose(1, 2, 0)
            dprob = jnp.einsum('qhed,khd->heqk', grad_f, value_f)
            dscore = lax.optimization_barrier((prob * (dprob - delta[..., None])).astype(jnp.bfloat16)).astype(jnp.float32)
            dquery = jnp.einsum('heqk,khd->qhed', dscore, key_f) * scale
            dkey = jnp.einsum('heqk,qhed->khd', dscore, query_f) * scale
            dvalue = jnp.einsum('heqk,qhed->khd', prob_r, grad_f)
            q_grad = rotate(dquery.reshape(BLK, HQ, HEAD), rows - row_start, -1.0).astype(jnp.bfloat16).reshape(BLK, QW)
            row_lse = lse[..., 0].transpose(2, 0, 1).reshape(BLK, HQ)
            kv_grad = jnp.concatenate([dkey.reshape(span, KW), dvalue.reshape(span, KW)], axis=1)
            return (attn.reshape(BLK, QW), q_grad, row_lse, kv_grad)

        def one_owner(running, device):
            slot = lax.optimization_barrier(jnp.sum(jnp.where(grid == device, counter[None, :], 0), axis=1)).astype(jnp.int32)
            firsts = counter * TOK_DEV + slot * BLK
            attn, q_grad, row_lse, kv_grad = jax.vmap(one_block)(firsts)

            def add_block(index, buffer):
                at_row = firsts[index]
                return lax.dynamic_update_slice_in_dim(buffer, lax.dynamic_slice_in_dim(buffer, at_row, span, 0) + kv_grad[index], at_row, 0)
            buffer = lax.fori_loop(0, N_CTX, add_block, jnp.zeros((WIN + SEQ, 2 * KW), jnp.float32))
            partial_value = lax.optimization_barrier(buffer[WIN:].astype(jnp.bfloat16)).astype(jnp.float32)
            return (running + partial_value, (attn, q_grad, row_lse, counter * N_CTX + slot))
        kv_total, (attn, q_grad, row_lse, blocks) = lax.scan(one_owner, jnp.zeros((SEQ, 2 * KW), jnp.float32), counter)
        flat = blocks.reshape(-1).astype(jnp.int32)
        attn_seq = jnp.zeros((NB, BLK, QW), jnp.bfloat16).at[flat].set(attn.reshape(NB, BLK, QW)).reshape(SEQ, QW)
        q_seq = jnp.zeros((NB, BLK, QW), jnp.bfloat16).at[flat].set(q_grad.reshape(NB, BLK, QW)).reshape(SEQ, QW)
        k_seq = rotate(kv_total[:, :KW].reshape(SEQ, KV_HEADS, HEAD), rel, -1.0).astype(jnp.bfloat16).reshape(SEQ, KW)
        v_seq = kv_total[:, KW:].astype(jnp.bfloat16)
        weight = lax.dot_general(attn_seq, seq_dy, (((0,), (0,)), ((), ())), preferred_element_type=jnp.float32)
        return (attn_seq, q_seq, k_seq, v_seq, row_lse.reshape(N_CTX, TOK_DEV, HQ), weight)
    attn, q_grad, k_grad, v_grad, stats, weights = lax.map(one_sequence, (queries, keys, values, doc_lengths, owner, out_grad))
    return (attn, q_grad, k_grad, v_grad, lax.optimization_barrier(jnp.sum(weights, axis=0)), stats)
```

```python
import functools
import math

import numpy as np

import jax
import jax.numpy as jnp
from jax import lax
from jax.experimental import pallas as pl
from jax.experimental.pallas import tpu as pltpu
from jax.sharding import PartitionSpec as P

HEAD = 128
WIN = 4096
NEG = -1e30
LOG2E = math.log2(math.e)
LN2 = math.log(2.0)
SCALE = 1.0 / math.sqrt(HEAD)
VMEM_LIMIT = 56 * 1024 * 1024
F32 = jnp.float32
BF16 = jnp.bfloat16


def doc_starts(lens_ref, pos):
    begin = jnp.int32(0)
    found = jnp.zeros_like(pos)
    for d in range(lens_ref.shape[1]):
        found = jnp.where(pos >= begin, begin, found)
        begin = begin + lens_ref[0, d]
    return found


def sincos(angle):
    turns = jnp.floor(angle * (2.0 / math.pi) + 0.5)
    rest = angle - turns * 1.5703125
    rest = rest - turns * 4.83751296997070312e-4
    rest = rest - turns * 7.54978995489188216e-8
    square = rest * rest
    sine = rest + rest * square * (
        -1.6666654611e-1 + square * (8.3321608736e-3 + square * -1.9515295891e-4)
    )
    cosine = (
        1.0
        - 0.5 * square
        + square
        * square
        * (4.166664568298827e-2 + square * (-1.388731625493765e-3 + square * 2.443315711809948e-5))
    )
    quarter = turns.astype(jnp.int32) & 3
    odd = (quarter & 1) == 1
    out_sin = jnp.where(odd, cosine, sine)
    out_cos = jnp.where(odd, sine, cosine)
    out_sin = jnp.where(quarter >= 2, -out_sin, out_sin)
    out_cos = jnp.where((quarter == 1) | (quarter == 2), -out_cos, out_cos)
    return out_sin, out_cos


def prep_kernel(meta_ref, lens_ref, freq_ref, q_ref, k_ref, qrot_ref, krot_ref, cos_ref, sin_ref):
    rows = q_ref.shape[0]
    pos = meta_ref[0] + lax.broadcasted_iota(jnp.int32, (rows, HEAD), 0)
    rel = pos - doc_starts(lens_ref, pos)
    sine, cosine = sincos(rel.astype(F32) * freq_ref[...])
    lane = lax.broadcasted_iota(jnp.int32, (rows, HEAD), 1)
    sine = jnp.where(lane < HEAD // 2, -sine, sine)
    cos_ref[...] = cosine
    sin_ref[...] = sine
    k = k_ref[...].astype(F32)
    krot_ref[...] = (k * cosine + pltpu.roll(k, HEAD // 2, 1) * sine).astype(BF16)
    for h in range(q_ref.shape[1] // HEAD):
        q = q_ref[:, h * HEAD : (h + 1) * HEAD].astype(F32)
        out = q * cosine + pltpu.roll(q, HEAD // 2, 1) * sine
        qrot_ref[:, h * HEAD : (h + 1) * HEAD] = out.astype(BF16)


def load_slots(meta_ref, refs, scratch, sem, rows):
    for start in (True, False):
        for i, ref in enumerate(refs):
            slot = meta_ref[2 + i]

            @pl.when(slot >= 0)
            def _():
                at = pl.multiple_of(slot * rows, rows)
                copy = pltpu.make_async_copy(ref, scratch.at[pl.ds(at, rows)], sem.at[i])
                if start:
                    copy.start()
                else:
                    copy.wait()


def key_range(meta_ref, lens_ref, first, qb, kb, slots_base):
    low = jnp.maximum(doc_starts(lens_ref, first), first - WIN + 1)
    lo_blk = jnp.maximum(low - slots_base, 0) // kb
    hi_blk = (first + qb - 1 - slots_base) // kb + 1
    return lo_blk, hi_blk


def fwd_kernel(n_refs, meta_ref, lens_ref, owner_ref, q_ref, *rest):
    k_refs, v_refs = rest[:n_refs], rest[n_refs : 2 * n_refs]
    o_ref, lse_ref, send_ref, s_scr, k_scr, v_scr, sem_k, sem_v = rest[2 * n_refs :]
    step = pl.program_id(0)
    qb, width = q_ref.shape
    heads = width // HEAD
    rows = heads * qb
    tok = k_refs[0].shape[0]
    kb = s_scr.shape[2]

    @pl.when(step == 0)
    def _():
        load_slots(meta_ref, k_refs, k_scr, sem_k, tok)
        load_slots(meta_ref, v_refs, v_scr, sem_v, tok)

    home = meta_ref[0]
    base = home - (k_scr.shape[0] - tok)
    first = home + step * qb
    q = jnp.concatenate([q_ref[:, h * HEAD : (h + 1) * HEAD] for h in range(heads)], axis=0)
    pos = first + lax.broadcasted_iota(jnp.int32, (qb, 1), 0)
    low = jnp.maximum(doc_starts(lens_ref, pos), pos - WIN + 1)
    pos_rows = jnp.concatenate([pos] * heads, axis=0)
    low_rows = jnp.concatenate([low] * heads, axis=0)
    lo_blk, hi_blk = key_range(meta_ref, lens_ref, first, qb, kb, base)

    def score(j, top):
        at = pl.multiple_of(j * kb, kb)
        k = k_scr[pl.ds(at, kb), :]
        s = lax.dot_general(q, k, (((1,), (1,)), ((), ())), preferred_element_type=F32)
        key = base + at + lax.broadcasted_iota(jnp.int32, (1, kb), 1)
        s = jnp.where((key >= low_rows) & (key <= pos_rows), s * (SCALE * LOG2E), NEG)
        s_scr[j] = s
        for c in range(kb // 128):
            top = jnp.maximum(top, s[:, c * 128 : (c + 1) * 128])
        return top

    top = lax.fori_loop(lo_blk, hi_blk, score, jnp.full((rows, 128), NEG, F32))
    top = jnp.max(top, axis=1, keepdims=True)

    def weigh(j, carry):
        total, acc = carry
        at = pl.multiple_of(j * kb, kb)
        p = jnp.exp2(s_scr[j] - top)
        for c in range(kb // 128):
            total = total + p[:, c * 128 : (c + 1) * 128]
        acc = acc + lax.dot_general(
            p.astype(BF16), v_scr[pl.ds(at, kb), :], (((1,), (0,)), ((), ())),
            preferred_element_type=F32,
        )
        return total, acc

    zero = jnp.zeros((rows, 128), F32)
    total, acc = lax.fori_loop(lo_blk, hi_blk, weigh, (zero, zero))
    total = jnp.sum(total, axis=1, keepdims=True)
    out = (acc / total).astype(BF16)
    lse = (top + jnp.log2(total)) * LN2
    for h in range(heads):
        o_ref[:, h * HEAD : (h + 1) * HEAD] = out[h * qb : (h + 1) * qb, :]
        wide = jnp.broadcast_to(lse[h * qb : (h + 1) * qb, :], (qb, 128))
        lse_ref[h : h + 1, :] = jnp.transpose(wide)[:1, :]
    block_len = send_ref.shape[2]
    for b in range(qb // block_len):
        to = owner_ref[meta_ref[1] + step * (qb // block_len) + b]
        send_ref[to] = lse_ref[:, b * block_len : (b + 1) * block_len]


def bwd_kernel(n_refs, kb, meta_ref, lens_ref, q_ref, dy_ref, o_ref, lse_ref, cos_ref, sin_ref, *rest):
    k_refs, v_refs = rest[:n_refs], rest[n_refs : 2 * n_refs]
    dq_ref, far_ref, own_ref, k_scr, v_scr, dk_scr, dv_scr, sem_k, sem_v = rest[2 * n_refs :]
    step = pl.program_id(0)
    qb, width = q_ref.shape
    heads = width // HEAD
    rows = heads * qb
    tok = k_refs[0].shape[0]

    @pl.when(step == 0)
    def _():
        load_slots(meta_ref, k_refs, k_scr, sem_k, tok)
        load_slots(meta_ref, v_refs, v_scr, sem_v, tok)
        dk_scr[...] = jnp.zeros_like(dk_scr)
        dv_scr[...] = jnp.zeros_like(dv_scr)

    home = meta_ref[0]
    base = home - (k_scr.shape[0] - tok)
    first = home + step * qb

    def stack(ref):
        return jnp.concatenate([ref[:, h * HEAD : (h + 1) * HEAD] for h in range(heads)], axis=0)

    q, dy = stack(q_ref), stack(dy_ref)
    prod = dy.astype(F32) * stack(o_ref).astype(F32)
    delta = jnp.concatenate(
        [
            jnp.sum(jnp.transpose(prod[h * qb : (h + 1) * qb, :]), axis=0, keepdims=True)
            for h in range(heads)
        ],
        axis=1,
    )
    lse = jnp.concatenate([lse_ref[h : h + 1, :] for h in range(heads)], axis=1) * LOG2E
    pos = first + lax.broadcasted_iota(jnp.int32, (1, qb), 1)
    low = jnp.maximum(doc_starts(lens_ref, pos), pos - WIN + 1)
    pos_rows = jnp.concatenate([pos] * heads, axis=1)
    low_rows = jnp.concatenate([low] * heads, axis=1)
    lo_blk, hi_blk = key_range(meta_ref, lens_ref, first, qb, kb, base)

    def visit(j, dq):
        at = pl.multiple_of(j * kb, kb)
        k = k_scr[pl.ds(at, kb), :]
        v = v_scr[pl.ds(at, kb), :]
        s = lax.dot_general(k, q, (((1,), (1,)), ((), ())), preferred_element_type=F32)
        dp = lax.dot_general(v, dy, (((1,), (1,)), ((), ())), preferred_element_type=F32)
        key = base + at + lax.broadcasted_iota(jnp.int32, (kb, 1), 0)
        s = jnp.where((key >= low_rows) & (key <= pos_rows), s * (SCALE * LOG2E) - lse, NEG)
        p = jnp.exp2(s)
        ds = (p * (dp - delta)).astype(BF16)
        dv_scr[pl.ds(at, kb), :] += lax.dot_general(
            p.astype(BF16), dy, (((1,), (0,)), ((), ())), preferred_element_type=F32
        )
        dk_scr[pl.ds(at, kb), :] += lax.dot_general(
            ds, q, (((1,), (0,)), ((), ())), preferred_element_type=F32
        )
        return dq + lax.dot_general(ds, k, (((0,), (0,)), ((), ())), preferred_element_type=F32)

    dq = lax.fori_loop(lo_blk, hi_blk, visit, jnp.zeros((rows, HEAD), F32)) * SCALE
    for h in range(heads):
        part = dq[h * qb : (h + 1) * qb, :]
        part = part * cos_ref[...] - pltpu.roll(part, HEAD // 2, 1) * sin_ref[...]
        dq_ref[:, h * HEAD : (h + 1) * HEAD] = part.astype(BF16)

    @pl.when(step == pl.num_programs(0) - 1)
    def _():
        for r in range(far_ref.shape[0]):
            far_ref[r, :, :HEAD] = dk_scr[r * tok : (r + 1) * tok, :].astype(BF16)
            far_ref[r, :, HEAD:] = dv_scr[r * tok : (r + 1) * tok, :].astype(BF16)
        own_ref[:, :HEAD] = dk_scr[far_ref.shape[0] * tok :, :]
        own_ref[:, HEAD:] = dv_scr[far_ref.shape[0] * tok :, :]


def wo_kernel(meta_ref, a_ref, g_ref, out_ref, at_scr):
    @pl.when(pl.program_id(0) == 0)
    def _():
        at_scr[...] = jnp.transpose(a_ref[...])

    col = out_ref.shape[3]
    res = jnp.dot(at_scr[...], g_ref[...], preferred_element_type=F32).astype(BF16)
    for j in range(out_ref.shape[1]):
        out_ref[0, j ^ meta_ref[1]] = res[:, j * col : (j + 1) * col]


def home_kernel(n_in, own_ref, cos_ref, sin_ref, *rest):
    ins, (dk_ref, dv_ref) = rest[:n_in], rest[n_in:]
    total = own_ref[...]
    for ref in ins:
        total = total + ref[...].astype(F32)
    dk = total[:, :HEAD] * SCALE
    dk = dk * cos_ref[...] - pltpu.roll(dk, HEAD // 2, 1) * sin_ref[...]
    dk_ref[...] = dk.astype(BF16)
    dv_ref[...] = total[:, HEAD:].astype(BF16)


SMEM_SPEC = pl.BlockSpec(memory_space=pltpu.SMEM)
VMEM_SPEC = pl.BlockSpec(memory_space=pltpu.VMEM)
ANY_SPEC = pl.BlockSpec(memory_space=pl.ANY)


def params():
    return pltpu.CompilerParams(
        dimension_semantics=("arbitrary",), vmem_limit_bytes=VMEM_LIMIT
    )


def on_device(queries, keys, values, doc_lengths, owner, out_weight, out_grad):
    n_ctx = lax.axis_size("ctx")
    n_dp = lax.axis_size("dp")
    dev = lax.axis_index("ctx").astype(jnp.int32)
    dp = lax.axis_index("dp").astype(jnp.int32)
    tok = queries.shape[1]
    width = queries.shape[2]
    heads = width // HEAD
    seq_len = tok * n_ctx
    block_len = tok // n_ctx
    d_model = out_grad.shape[2]
    reach = min(WIN, seq_len // 2)
    back = min(-(-reach // tok), n_ctx - 1)
    home_pos = dev * tok
    sds = jax.ShapeDtypeStruct

    half = HEAD // 2
    freq = (10000.0 ** (-2.0 * np.arange(half) / HEAD)).astype(np.float32)
    freq = jnp.asarray(np.concatenate([freq, freq])[None, :])

    def shift(x, pairs):
        return lax.ppermute(x, "ctx", pairs)

    paired = n_ctx == 8 and back == 4
    hop = [(i, i + 2) for i in range(n_ctx - 2)]
    hop_back = [(b, a) for a, b in hop]
    up = [(i, i + 1) for i in range(0, n_ctx, 2)]
    down = [(b, a) for a, b in up]
    swap = up + down
    odd = dev % 2

    def collect(x):
        if paired:
            a1 = shift(x, hop)
            e1 = shift(x, up)
            a2 = shift(a1, hop)
            s1 = shift(a1, swap)
            o3 = shift(a2, down)
            return [x, a1, e1, a2, s1, o3]
        return [x] + [
            shift(x, [(i, i + s) for i in range(n_ctx - s)]) for s in range(1, back + 1)
        ]

    if paired:
        skip = jnp.int32(-1)
        slots = [
            jnp.int32(4),
            jnp.int32(2),
            jnp.where(odd == 1, 3, skip),
            jnp.int32(0),
            jnp.where(odd == 1, 1, 3),
            jnp.where(odd == 1, skip, 1),
        ]
    else:
        slots = [jnp.int32(back - s) for s in range(back + 1)]
    meta = jnp.stack([home_pos, dev * n_ctx] + [jnp.asarray(s, jnp.int32) for s in slots])
    meta_wo = jnp.stack([dp, dev])

    v_blocks = collect(values[0])

    q_rot, k_rot, cos, sin = pl.pallas_call(
        prep_kernel,
        out_shape=(
            sds((tok, width), BF16),
            sds((tok, HEAD), BF16),
            sds((tok, HEAD), F32),
            sds((tok, HEAD), F32),
        ),
        in_specs=[SMEM_SPEC, SMEM_SPEC, VMEM_SPEC, VMEM_SPEC, VMEM_SPEC],
        out_specs=(VMEM_SPEC,) * 4,
        compiler_params=pltpu.CompilerParams(vmem_limit_bytes=VMEM_LIMIT),
        name="prep",
    )(meta, doc_lengths, freq, queries[0], keys[0])
    k_blocks = collect(k_rot)

    d_out = lax.dot_general(
        out_grad[0], out_weight, (((1,), (1,)), ((), ())), preferred_element_type=F32
    ).astype(BF16)

    n_refs = len(k_blocks)
    n_keys = (back + 1) * tok
    qb = 128
    kb = min(512, tok)
    tok_spec = pl.BlockSpec((qb, width), lambda i: (i, 0))
    lse_spec = pl.BlockSpec((heads, qb), lambda i: (0, i))
    table_spec = pl.BlockSpec((qb, HEAD), lambda i: (i, 0))
    kv_scratch = [pltpu.VMEM((n_keys, HEAD), BF16), pltpu.VMEM((n_keys, HEAD), BF16)]
    sems = [pltpu.SemaphoreType.DMA((n_refs,)), pltpu.SemaphoreType.DMA((n_refs,))]
    pair_flops = 2 * heads * tok * (tok + reach // 2) * HEAD
    attn, lse, lse_send = pl.pallas_call(
        functools.partial(fwd_kernel, n_refs),
        grid=(tok // qb,),
        out_shape=(
            sds((tok, width), BF16),
            sds((heads, tok), F32),
            sds((n_ctx, heads, block_len), F32),
        ),
        in_specs=[SMEM_SPEC, SMEM_SPEC, SMEM_SPEC, tok_spec] + [ANY_SPEC] * (2 * n_refs),
        out_specs=(tok_spec, lse_spec, pl.BlockSpec((n_ctx, heads, block_len), lambda i: (0, 0, 0))),
        scratch_shapes=[pltpu.VMEM((n_keys // kb, heads * qb, kb), F32)] + kv_scratch + sems,
        compiler_params=params(),
        cost_estimate=pl.CostEstimate(
            flops=4 * pair_flops, bytes_accessed=4 << 20, transcendentals=pair_flops // HEAD
        ),
        name="fwd",
    )(meta, doc_lengths, owner[0], q_rot, *k_blocks, *v_blocks)

    lse_recv = lax.all_to_all(lse_send, "ctx", split_axis=0, concat_axis=0, tiled=True)
    owner_lse = lse_recv.transpose(0, 2, 1).reshape(1, 1, tok, heads)

    col = d_model // (n_dp * n_ctx)
    bits_dp = n_dp.bit_length() - 1
    bits_ctx = n_ctx.bit_length() - 1

    def partial_wo(part, core, rows):
        return pl.pallas_call(
            wo_kernel,
            grid_spec=pltpu.PrefetchScalarGridSpec(
                num_scalar_prefetch=1,
                grid=(n_dp // 2,),
                in_specs=[
                    pl.BlockSpec((tok, rows), lambda i, m: (0, part)),
                    pl.BlockSpec((tok, n_ctx * col), lambda i, m: (0, (2 * i + core) ^ m[0])),
                ],
                out_specs=pl.BlockSpec((1, n_ctx, rows, col), lambda i, m: (i, 0, 0, 0)),
                scratch_shapes=[pltpu.VMEM((rows, tok), BF16)],
            ),
            out_shape=sds((n_dp // 2, n_ctx, rows, col), BF16),
            compiler_params=params(),
            cost_estimate=pl.CostEstimate(
                flops=tok * rows * d_model, bytes_accessed=6 << 20, transcendentals=0
            ),
            name="wo",
        )(meta_wo, attn, out_grad[0])

    def exchange(x, axis, bit, size):
        return lax.ppermute(x, axis, [(i, i ^ bit) for i in range(size)])

    n_parts = 2
    rows = width // n_parts
    reduced = []
    for part in range(n_parts):
        send = partial_wo(part, 1, rows)
        recv = exchange(send, "dp", 1, n_dp)
        keep = partial_wo(part, 0, rows)
        shape = (2,) * (bits_dp - 1 + bits_ctx) + (rows, col)
        pieces = (keep.reshape(shape), recv.reshape(shape))
        left = [("dp", b) for b in range(bits_dp - 1, 0, -1)]
        left += [("ctx", b) for b in range(bits_ctx - 1, -1, -1)]
        order = [("dp", b) for b in range(1, bits_dp)]
        if part == 0:
            order = order + [("ctx", b) for b in range(bits_ctx)]
        else:
            order = [("ctx", 0)] + order + [("ctx", b) for b in range(1, bits_ctx)]
        for axis, b in order:
            at = left.index((axis, b))
            left.pop(at)

            def pick(which):
                one, two = [lax.index_in_dim(x, which, at, keepdims=False) for x in pieces]
                return (one.astype(F32) + two.astype(F32)).astype(BF16)

            send = pick(1)
            recv = exchange(send, axis, 1 << b, n_dp if axis == "dp" else n_ctx)
            pieces = (pick(0), recv)
        reduced.append(pieces[0].astype(F32) + pieces[1].astype(F32))
    wgrad = jnp.concatenate(reduced, axis=0)

    q_grad, far, own = pl.pallas_call(
        functools.partial(bwd_kernel, n_refs, kb),
        grid=(tok // qb,),
        out_shape=(
            sds((tok, width), BF16),
            sds((back, tok, 2 * HEAD), BF16),
            sds((tok, 2 * HEAD), F32),
        ),
        in_specs=[SMEM_SPEC, SMEM_SPEC, tok_spec, tok_spec, tok_spec, lse_spec, table_spec, table_spec]
        + [ANY_SPEC] * (2 * n_refs),
        out_specs=(
            tok_spec,
            pl.BlockSpec((back, tok, 2 * HEAD), lambda i: (0, 0, 0)),
            pl.BlockSpec((tok, 2 * HEAD), lambda i: (0, 0)),
        ),
        scratch_shapes=kv_scratch
        + [pltpu.VMEM((n_keys, HEAD), F32), pltpu.VMEM((n_keys, HEAD), F32)]
        + sems,
        compiler_params=params(),
        cost_estimate=pl.CostEstimate(
            flops=8 * pair_flops, bytes_accessed=8 << 20, transcendentals=pair_flops // HEAD
        ),
        name="bwd",
    )(meta, doc_lengths, q_rot, d_out, attn, lse, cos, sin, *k_blocks, *v_blocks)

    def plus(*xs):
        return functools.reduce(jnp.add, [x.astype(F32) for x in xs]).astype(BF16)

    if paired:
        d4, d3, d2, d1 = far[0], far[1], far[2], far[3]
        sum4 = plus(d4, shift(d3, up))
        b2 = shift(sum4, hop_back)
        s1 = shift(jnp.where(odd == 1, d3, d1), swap)
        sum2 = plus(d2, b2, s1)
        arrived = [shift(sum2, hop_back), shift(d1, down)]
    else:
        arrived = [
            shift(far[back - s], [(i + s, i) for i in range(n_ctx - s)]) for s in range(1, back + 1)
        ]
    k_grad, v_grad = pl.pallas_call(
        functools.partial(home_kernel, len(arrived)),
        out_shape=(sds((tok, HEAD), BF16), sds((tok, HEAD), BF16)),
        in_specs=[VMEM_SPEC] * (3 + len(arrived)),
        out_specs=(VMEM_SPEC, VMEM_SPEC),
        compiler_params=pltpu.CompilerParams(vmem_limit_bytes=VMEM_LIMIT),
        name="home",
    )(own, cos, sin, *arrived)

    return (attn[None], q_grad[None], k_grad[None], v_grad[None], wgrad, owner_lse)


def solution(mesh):
    in_specs = (
        P("dp", "ctx", None),
        P("dp", "ctx", None),
        P("dp", "ctx", None),
        P("dp", None),
        P("dp", None),
        P(),
        P("dp", "ctx", None),
    )
    out_specs = (
        P("dp", "ctx", None),
        P("dp", "ctx", None),
        P("dp", "ctx", None),
        P("dp", "ctx", None),
        P(None, ("dp", "ctx")),
        P("dp", "ctx", None, None),
    )
    return jax.shard_map(
        on_device, mesh=mesh, in_specs=in_specs, out_specs=out_specs, check_vma=False
    )
```

```python
import functools
import math

import numpy as np

import jax
import jax.numpy as jnp
from jax import lax
from jax.experimental import pallas as pl
from jax.experimental.pallas import tpu as pltpu
from jax.sharding import PartitionSpec as P

HEAD = 128
WIN = 4096
NEG = -1e30
LOG2E = math.log2(math.e)
LN2 = math.log(2.0)
SCALE = 1.0 / math.sqrt(HEAD)
F32 = jnp.float32
BF16 = jnp.bfloat16


def doc_starts(lens_ref, pos):
    begin = jnp.int32(0)
    found = jnp.zeros_like(pos)
    for d in range(lens_ref.shape[1]):
        found = jnp.where(pos >= begin, begin, found)
        begin = begin + lens_ref[0, d]
    return found


def sincos(angle):
    turns = jnp.floor(angle * (2.0 / math.pi) + 0.5)
    rest = angle - turns * 1.5703125
    rest = rest - turns * 4.83751296997070312e-4
    rest = rest - turns * 7.54978995489188216e-8
    square = rest * rest
    sine = rest + rest * square * (
        -1.6666654611e-1 + square * (8.3321608736e-3 + square * -1.9515295891e-4)
    )
    cosine = (
        1.0
        - 0.5 * square
        + square
        * square
        * (4.166664568298827e-2 + square * (-1.388731625493765e-3 + square * 2.443315711809948e-5))
    )
    quarter = turns.astype(jnp.int32) & 3
    odd = (quarter & 1) == 1
    out_sin = jnp.where(odd, cosine, sine)
    out_cos = jnp.where(odd, sine, cosine)
    out_sin = jnp.where(quarter >= 2, -out_sin, out_sin)
    out_cos = jnp.where((quarter == 1) | (quarter == 2), -out_cos, out_cos)
    return out_sin, out_cos


def place():
    return lax.axis_index("ctx").astype(jnp.int32), lax.axis_size("ctx")


def rotate(x, cosine, sine):
    return x * cosine + pltpu.roll(x, HEAD // 2, 1) * sine


def prep_kernel(lens_ref, freq_ref, k_ref, v_ref, kv_ref, cos_ref, sin_ref):
    rows = k_ref.shape[0]
    dev, _ = place()
    pos = dev * rows + lax.broadcasted_iota(jnp.int32, (rows, HEAD), 0)
    rel = pos - doc_starts(lens_ref, pos)
    sine, cosine = sincos(rel.astype(F32) * freq_ref[...])
    lane = lax.broadcasted_iota(jnp.int32, (rows, HEAD), 1)
    sine = jnp.where(lane < HEAD // 2, -sine, sine)
    cos_ref[...] = cosine
    sin_ref[...] = sine
    kv_ref[:, :HEAD] = rotate(k_ref[...].astype(F32), cosine, sine).astype(BF16)
    kv_ref[:, HEAD:] = v_ref[...]


def rotq_kernel(q_ref, cos_ref, sin_ref, out_ref):
    for h in range(q_ref.shape[1] // HEAD):
        q = q_ref[:, h * HEAD : (h + 1) * HEAD].astype(F32)
        out_ref[:, h * HEAD : (h + 1) * HEAD] = rotate(q, cos_ref[...], sin_ref[...]).astype(BF16)


def is_paired(n_ctx, back):
    return n_ctx == 8 and back == 4


def slot_list(dev, n_ctx, back):
    if is_paired(n_ctx, back):
        odd = dev % 2 == 1
        skip = jnp.int32(-1)
        return [4, 2, jnp.where(odd, 3, skip), 0, jnp.where(odd, 1, 3), jnp.where(odd, skip, 1)]
    return [back - s for s in range(back + 1)]


def load_slots(slots, refs, scratch, sem, rows, lo=0):
    hi = lo + scratch.shape[0] // rows
    for start in (True, False):
        for i, (slot, ref) in enumerate(zip(slots, refs)):
            if isinstance(slot, int) and not lo <= slot < hi:
                continue

            def move(slot=slot, ref=ref, i=i):
                at = (slot - lo) * rows
                if not isinstance(at, int):
                    at = pl.multiple_of(at, rows)
                copy = pltpu.make_async_copy(ref, scratch.at[pl.ds(at, rows)], sem.at[i])
                if start:
                    copy.start()
                else:
                    copy.wait()

            if isinstance(slot, int):
                move()
            else:
                pl.when((slot >= lo) & (slot < hi))(move)


def tile_ranges(lens_ref, first, qb, kb, base, n_tiles):
    last = first + qb - 1
    low_first = jnp.maximum(doc_starts(lens_ref, first), first - WIN + 1)
    low_last = jnp.maximum(doc_starts(lens_ref, last), last - WIN + 1)
    hi = jnp.minimum((last - base) // kb + 1, n_tiles)
    lo = jnp.minimum(jnp.maximum(low_first - base, 0) // kb, hi)
    full_lo = jnp.clip((jnp.maximum(low_last - base, 0) + kb - 1) // kb, lo, hi)
    full_hi = jnp.clip((first - base + 1) // kb, full_lo, hi)
    return lo, full_lo, full_hi, hi


def over_tiles(ranges, visit, carry):
    lo, full_lo, full_hi, hi = ranges
    carry = lax.fori_loop(full_lo, full_hi, functools.partial(visit, False), carry)

    def edge(i, c):
        return visit(True, jnp.where(lo + i < full_lo, lo + i, full_hi + i - (full_lo - lo)), c)

    return lax.fori_loop(0, (full_lo - lo) + (hi - full_hi), edge, carry)


def fold(x, op):
    return op(x.reshape(x.shape[0] // 8, 8, x.shape[1]), axis=0)


def stack_heads(ref):
    heads = ref.shape[1] // HEAD
    return jnp.concatenate([ref[:, h * HEAD : (h + 1) * HEAD] for h in range(heads)], axis=0)


def query_bounds(lens_ref, first, qb, heads):
    pos = first + lax.broadcasted_iota(jnp.int32, (1, qb), 1)
    low = jnp.maximum(doc_starts(lens_ref, pos), pos - WIN + 1)
    return jnp.concatenate([low] * heads, axis=1), jnp.concatenate([pos] * heads, axis=1)


def masked_scores(s, base, at, low, high):
    key = base + at + lax.broadcasted_iota(jnp.int32, (s.shape[0], 1), 0)
    return jnp.where((key >= low) & (key <= high), s, NEG)


NT = (((1,), (1,)), ((), ()))
NN = (((1,), (0,)), ((), ()))
TN = (((0,), (0,)), ((), ()))


def dot(a, b, dims):
    return lax.dot_general(a, b, dims, preferred_element_type=F32)


def fwd_kernel(n_refs, back, kb, lens_ref, q_ref, *rest):
    kv_refs = rest[:n_refs]
    o_ref, lse_ref, pack_ref, kv_scr, sem = rest[n_refs:]
    step = pl.program_id(0)
    qb, width = q_ref.shape
    heads = width // HEAD
    rows = heads * qb
    tok = kv_refs[0].shape[0]
    dev, n_ctx = place()

    @pl.when(step == 0)
    def _():
        load_slots(slot_list(dev, n_ctx, back), kv_refs, kv_scr, sem, tok)

    base = (dev - back) * tok
    first = dev * tok + step * qb
    q = stack_heads(q_ref)
    low, high = query_bounds(lens_ref, first, qb, heads)
    factor = SCALE * LOG2E

    def visit(masked, j, carry):
        top, total, acc = carry
        at = pl.multiple_of(j * kb, kb)
        s = dot(kv_scr[pl.ds(at, kb), :HEAD], q, NT)
        if masked:
            s = masked_scores(s, base, at, low, high)
        new = jnp.maximum(top, jnp.max(fold(s, jnp.max), axis=0, keepdims=True) * factor)
        alpha = jnp.exp2(top - new)
        p = jnp.exp2(s * factor - new)
        total = total * alpha + fold(p, jnp.sum)
        acc = acc * alpha + dot(kv_scr[pl.ds(at, kb), HEAD:], p.astype(BF16), TN)
        return new, total, acc

    carry = (jnp.full((1, rows), NEG, F32), jnp.zeros((8, rows), F32), jnp.zeros((HEAD, rows), F32))
    ranges = tile_ranges(lens_ref, first, qb, kb, base, kv_scr.shape[0] // kb)
    top, total, acc = over_tiles(ranges, visit, carry)
    total = jnp.sum(total, axis=0, keepdims=True)
    lse = (top + jnp.log2(total)) * LN2
    out = acc / total
    for h in range(heads):
        lse_ref[h : h + 1, :] = lse[:, h * qb : (h + 1) * qb]
        o_ref[:, h * HEAD : (h + 1) * HEAD] = jnp.transpose(out[:, h * qb : (h + 1) * qb]).astype(BF16)
    lines = jnp.concatenate(
        [lse[:, c * HEAD : (c + 1) * HEAD] for c in range(rows // HEAD)], axis=0
    )
    coarse = lines.astype(BF16)
    fine = (lines - coarse.astype(F32)).astype(BF16)
    pack_ref[0] = jnp.concatenate([coarse, fine], axis=0)


def bwd_core(lens_ref, q_ref, dy_ref, o_ref, lse_ref, kv, base, kb, dk_scr, dv_scr, dq):
    qb, width = q_ref.shape
    heads = width // HEAD
    tok = qb * pl.num_programs(0)
    dev, _ = place()
    first = dev * tok + pl.program_id(0) * qb
    q, dy = stack_heads(q_ref), stack_heads(dy_ref)
    prod = dy.astype(F32) * stack_heads(o_ref).astype(F32)
    delta = jnp.concatenate(
        [
            jnp.sum(jnp.transpose(prod[h * qb : (h + 1) * qb, :]), axis=0, keepdims=True)
            for h in range(heads)
        ],
        axis=1,
    )
    lse = jnp.concatenate([lse_ref[h : h + 1, :] for h in range(heads)], axis=1) * LOG2E
    low, high = query_bounds(lens_ref, first, qb, heads)
    factor = SCALE * LOG2E

    def visit(masked, j, dq):
        at = pl.multiple_of(j * kb, kb)
        k, v = kv[pl.ds(at, kb), :HEAD], kv[pl.ds(at, kb), HEAD:]
        s = dot(k, q, NT)
        if masked:
            s = masked_scores(s, base, at, low, high)
        p = jnp.exp2(s * factor - lse)
        ds = (p * (dot(v, dy, NT) - delta)).astype(BF16)
        dv_scr[pl.ds(at, kb), :] += dot(p.astype(BF16), dy, NN)
        dk_scr[pl.ds(at, kb), :] += dot(ds, q, NN)
        return dq + dot(k, ds, TN)

    return over_tiles(tile_ranges(lens_ref, first, qb, kb, base, kv.shape[0] // kb), visit, dq)


def far_kernel(n_refs, back, lo, has_dq, kb, lens_ref, q_ref, dy_ref, o_ref, lse_ref, *rest):
    kv_refs = rest[:n_refs]
    dqin_ref = rest[n_refs] if has_dq else None
    dq_ref, far_ref, kv_scr, dk_scr, dv_scr, sem = rest[n_refs + has_dq :]
    tok = kv_refs[0].shape[0]
    dev, n_ctx = place()
    step = pl.program_id(0)

    @pl.when(step == 0)
    def _():
        load_slots(slot_list(dev, n_ctx, back)[1:], kv_refs, kv_scr, sem, tok, lo)
        dk_scr[...] = jnp.zeros_like(dk_scr)
        dv_scr[...] = jnp.zeros_like(dv_scr)

    base = (dev - back + lo) * tok
    dq = dqin_ref[0] if has_dq else jnp.zeros(dq_ref.shape[1:], F32)
    dq_ref[0] = bwd_core(
        lens_ref, q_ref, dy_ref, o_ref, lse_ref, kv_scr, base, kb, dk_scr, dv_scr, dq
    )

    @pl.when(step == pl.num_programs(0) - 1)
    def _():
        for r in range(far_ref.shape[0]):
            far_ref[r, :, :HEAD] = dk_scr[r * tok : (r + 1) * tok, :].astype(BF16)
            far_ref[r, :, HEAD:] = dv_scr[r * tok : (r + 1) * tok, :].astype(BF16)


def near_kernel(kb, lens_ref, q_ref, dy_ref, o_ref, lse_ref, dqin_ref, kv_ref, cos_ref, sin_ref,
                dq_ref, own_ref, dk_scr, dv_scr):
    tok = kv_ref.shape[0]
    dev, _ = place()
    step = pl.program_id(0)
    qb = q_ref.shape[0]

    @pl.when(step == 0)
    def _():
        dk_scr[...] = jnp.zeros_like(dk_scr)
        dv_scr[...] = jnp.zeros_like(dv_scr)

    dq = bwd_core(
        lens_ref, q_ref, dy_ref, o_ref, lse_ref, kv_ref, dev * tok, kb, dk_scr, dv_scr, dqin_ref[0]
    )
    for h in range(q_ref.shape[1] // HEAD):
        part = jnp.transpose(dq[:, h * qb : (h + 1) * qb]) * SCALE
        dq_ref[:, h * HEAD : (h + 1) * HEAD] = rotate(part, cos_ref[...], -sin_ref[...]).astype(BF16)

    @pl.when(step == pl.num_programs(0) - 1)
    def _():
        own_ref[:, :HEAD] = dk_scr[...]
        own_ref[:, HEAD:] = dv_scr[...]


def wo_kernel(core, group, a_ref, g_ref, *rest):
    outs, (g_scr, sem) = rest[:-2], rest[-2:]
    dev, _ = place()
    dp = lax.axis_index("dp").astype(jnp.int32)
    n_half, n_ctx, rows, col = outs[0].shape
    wide = group * col
    groups = n_ctx // group
    at = jnp.transpose(a_ref[...])

    def fetch(n):
        i, p = divmod(n, groups)
        block = ((2 * i + core) ^ dp) * groups + (p ^ (dev // group))
        start = pl.multiple_of(block * wide, wide)
        return pltpu.make_async_copy(g_ref.at[:, pl.ds(start, wide)], g_scr.at[n], sem.at[n])

    for n in range(n_half * groups):
        fetch(n).start()
    for n in range(n_half * groups):
        i, p = divmod(n, groups)
        fetch(n).wait()
        res = jnp.dot(at, g_scr[n], preferred_element_type=F32).astype(BF16)
        for j in range(group):
            to = p * group + (j ^ (dev & (group - 1)))
            for c, out_ref in enumerate(outs):
                out_ref[i, to] = res[c * rows : (c + 1) * rows, j * col : (j + 1) * col]


def home_kernel(n_in, own_ref, cos_ref, sin_ref, *rest):
    ins, (dk_ref, dv_ref) = rest[:n_in], rest[n_in:]
    total = own_ref[...]
    for ref in ins:
        total = total + ref[...].astype(F32)
    dk_ref[...] = rotate(total[:, :HEAD] * SCALE, cos_ref[...], -sin_ref[...]).astype(BF16)
    dv_ref[...] = total[:, HEAD:].astype(BF16)


def owner_kernel(owner_ref, lse_ref, out_ref):
    dev, n_ctx = place()
    heads = out_ref.shape[1]
    tok = out_ref.shape[0]
    block_len = tok // n_ctx
    halves = lse_ref.shape[1]
    chunks = tok // halves // HEAD
    for i in range(n_ctx):
        c = dev ^ i
        mine = jnp.zeros((heads, block_len), F32)
        lines = lse_ref[i].astype(F32)
        lines = lines[:, : heads * chunks] + lines[:, heads * chunks :]
        for s in range(n_ctx):
            half, rest = divmod(s * block_len, tok // halves)
            chunk, lane = divmod(rest, HEAD)
            part = jnp.concatenate(
                [
                    lines[half, h * chunks + chunk : h * chunks + chunk + 1, lane : lane + block_len]
                    for h in range(heads)
                ],
                axis=0,
            )
            mine = jnp.where(owner_ref[c * n_ctx + s] == dev, part, mine)
        out_ref[pl.ds(pl.multiple_of(c * block_len, block_len), block_len), :] = jnp.transpose(mine)


SMEM_SPEC = pl.BlockSpec(memory_space=pltpu.SMEM)
VMEM_SPEC = pl.BlockSpec(memory_space=pltpu.VMEM)
ANY_SPEC = pl.BlockSpec(memory_space=pl.ANY)


def params(mib, *semantics):
    return pltpu.CompilerParams(dimension_semantics=semantics or None, vmem_limit_bytes=mib << 20)


def cost(flops, size, exps=0):
    return pl.CostEstimate(flops=int(flops), bytes_accessed=int(size), transcendentals=int(exps))


def after(x, *others):
    return lax.optimization_barrier((x, *others))[0]


def on_device(queries, keys, values, doc_lengths, owner, out_weight, out_grad):
    n_ctx = lax.axis_size("ctx")
    n_dp = lax.axis_size("dp")
    dev = lax.axis_index("ctx").astype(jnp.int32)
    dp = lax.axis_index("dp").astype(jnp.int32)
    tok = queries.shape[1]
    width = queries.shape[2]
    heads = width // HEAD
    seq_len = tok * n_ctx
    d_model = out_grad.shape[2]
    reach = min(WIN, seq_len // 2)
    back = min(-(-reach // tok), n_ctx - 1)
    sds = jax.ShapeDtypeStruct

    half = HEAD // 2
    freq = (10000.0 ** (-2.0 * np.arange(half) / HEAD)).astype(np.float32)
    freq = jnp.asarray(np.concatenate([freq, freq])[None, :])

    def shift(x, pairs):
        return lax.ppermute(x, "ctx", pairs)

    hop = [(i, i + 2) for i in range(n_ctx - 2)]
    hop_back = [(b, a) for a, b in hop]
    up = [(i, i + 1) for i in range(0, n_ctx, 2)]
    down = [(b, a) for a, b in up]
    swap = up + down
    odd = dev % 2 == 1
    paired = is_paired(n_ctx, back)

    kv_home, cos, sin = pl.pallas_call(
        prep_kernel,
        out_shape=(sds((tok, 2 * HEAD), BF16), sds((tok, HEAD), F32), sds((tok, HEAD), F32)),
        in_specs=[SMEM_SPEC] + [VMEM_SPEC] * 3,
        out_specs=(VMEM_SPEC,) * 3,
        compiler_params=params(58),
        cost_estimate=cost(1 << 22, 1 << 20),
        name="prep",
    )(doc_lengths, freq, keys[0], values[0])

    def d_out_of(grad):
        return lax.dot_general(
            grad, out_weight, (((1,), (1,)), ((), ())), preferred_element_type=F32
        ).astype(BF16)

    def rotated_queries(x):
        return pl.pallas_call(
            rotq_kernel,
            out_shape=sds((tok, width), BF16),
            in_specs=[VMEM_SPEC] * 3,
            out_specs=VMEM_SPEC,
            compiler_params=params(4),
            cost_estimate=cost(1 << 22, 2 << 20),
            name="rotq",
        )(x, cos, sin)

    if paired:
        a1 = shift(kv_home, hop)
        e1 = shift(kv_home, up)
        d_out = d_out_of(out_grad[0])
        a1 = after(a1, d_out)
        s1 = shift(a1, swap)
        a2 = shift(a1, hop)
        q_rot = rotated_queries(queries[0])
        o3 = shift(a2, down)
        blocks = [kv_home, a1, e1, a2, s1, o3]
    else:
        blocks = [kv_home] + [
            shift(kv_home, [(i, i + s) for i in range(n_ctx - s)]) for s in range(1, back + 1)
        ]
        q_rot = rotated_queries(queries[0])
        d_out = d_out_of(out_grad[0])

    n_keys = (back + 1) * tok
    qb = tok // 2
    kb = tok
    tok_spec = pl.BlockSpec((qb, width), lambda i: (i, 0))
    lse_spec = pl.BlockSpec((heads, qb), lambda i: (0, i))
    table_spec = pl.BlockSpec((qb, HEAD), lambda i: (i, 0))
    dq_spec = pl.BlockSpec((1, HEAD, heads * qb), lambda i: (i, 0, 0))
    pairs = heads * tok * (tok + reach) // 2
    pack_rows = 2 * heads * qb // HEAD
    attn, lse, pack = pl.pallas_call(
        functools.partial(fwd_kernel, len(blocks), back, kb),
        grid=(tok // qb,),
        out_shape=(
            sds((tok, width), BF16),
            sds((heads, tok), F32),
            sds((tok // qb, pack_rows, HEAD), BF16),
        ),
        in_specs=[SMEM_SPEC, tok_spec] + [ANY_SPEC] * len(blocks),
        out_specs=(tok_spec, lse_spec, pl.BlockSpec((1, pack_rows, HEAD), lambda i: (i, 0, 0))),
        scratch_shapes=[
            pltpu.VMEM((n_keys, 2 * HEAD), BF16),
            pltpu.SemaphoreType.DMA((len(blocks),)),
        ],
        compiler_params=params(20, "arbitrary"),
        cost_estimate=cost(4 * pairs * HEAD, 4 << 20, pairs),
        name="fwd",
    )(doc_lengths, q_rot, *blocks)

    col = d_model // (n_dp * n_ctx)
    bits_dp = n_dp.bit_length() - 1
    bits_ctx = n_ctx.bit_length() - 1
    group = min(n_ctx, max(1, 256 // col))
    colors = 2
    rows = width // colors
    steps = n_dp // 2 * (n_ctx // group)

    def partial_wo(core):
        return pl.pallas_call(
            functools.partial(wo_kernel, core, group),
            out_shape=(sds((n_dp // 2, n_ctx, rows, col), BF16),) * colors,
            in_specs=[VMEM_SPEC, ANY_SPEC],
            out_specs=(VMEM_SPEC,) * colors,
            scratch_shapes=[
                pltpu.VMEM((steps, tok, group * col), BF16),
                pltpu.SemaphoreType.DMA((steps,)),
            ],
            compiler_params=params(16),
            cost_estimate=cost(tok * width * d_model, 6 << 20),
            name="wo",
        )(attn, out_grad[0])

    def exchange(x, axis, bit, size):
        return lax.ppermute(x, axis, [(i, i ^ bit) for i in range(size)])

    size_of = {"dp": n_dp, "ctx": n_ctx}
    lead = [("dp", b) for b in range(bits_dp - 1, 0, -1)]
    lead += [("ctx", b) for b in range(bits_ctx - 1, -1, -1)]

    class Parts:
        def __init__(self, one, two, left):
            self.one, self.two, self.left = one, two, left

        def pick(self, axis, which):
            at = self.left.index(axis)
            one, two = [lax.index_in_dim(x, which, at, keepdims=False) for x in (self.one, self.two)]
            return (one.astype(F32) + two.astype(F32)).astype(BF16)

        def step(self, axis, recv):
            left = [a for a in self.left if a != axis]
            return Parts(self.pick(axis, 0), recv, left)

    def move(x, axis):
        return exchange(x, axis[0], 1 << axis[1], size_of[axis[0]])

    wo_send = partial_wo(1)
    wo_recv = [exchange(x, "dp", 1, n_dp) for x in wo_send]
    wo_keep = partial_wo(0)
    shape = (2,) * len(lead) + (rows, col)
    color = [Parts(k.reshape(shape), r.reshape(shape), lead) for k, r in zip(wo_keep, wo_recv)]
    first_dp = [("dp", b) for b in range(1, bits_dp)]
    ctx_axes = [("ctx", b) for b in range(bits_ctx)]
    orders = [first_dp + ctx_axes[:1], ctx_axes[:1] + first_dp]

    lines = pack.reshape(-1, col)

    def move_with_lse(x, axis, lse_of):
        size = x.size // col
        out = move(jnp.concatenate([x.reshape(size, col), lse_of], axis=0), axis)
        return out[:size].reshape(x.shape), jnp.concatenate([lse_of, out[size:]], axis=0)

    sends = [color[c].pick(orders[c][0], 1) for c in range(colors)]
    recvs = [move(sends[0], orders[0][0])]
    recv, lines = move_with_lse(sends[1], orders[1][0], lines)
    recvs.append(recv)
    color = [color[c].step(orders[c][0], recvs[c]) for c in range(colors)]

    def backward_far(lo, hi, lse_in, dq_in):
        count = hi - lo
        return pl.pallas_call(
            functools.partial(far_kernel, len(blocks) - 1, back, lo, len(dq_in), kb),
            grid=(tok // qb,),
            out_shape=(sds((tok // qb, HEAD, heads * qb), F32), sds((count, tok, 2 * HEAD), BF16)),
            in_specs=[SMEM_SPEC, tok_spec, tok_spec, tok_spec, lse_spec]
            + [ANY_SPEC] * (len(blocks) - 1)
            + [dq_spec] * len(dq_in),
            out_specs=(dq_spec, pl.BlockSpec((count, tok, 2 * HEAD), lambda i: (0, 0, 0))),
            scratch_shapes=[
                pltpu.VMEM((count * tok, 2 * HEAD), BF16),
                pltpu.VMEM((count * tok, HEAD), F32),
                pltpu.VMEM((count * tok, HEAD), F32),
                pltpu.SemaphoreType.DMA((len(blocks) - 1,)),
            ],
            compiler_params=params(28, "arbitrary"),
            cost_estimate=cost(8 * pairs * HEAD, 8 << 20, pairs),
            name="far",
        )(doc_lengths, q_rot, d_out, attn, lse_in, *blocks[1:], *dq_in)

    def plus(*xs):
        return functools.reduce(jnp.add, [x.astype(F32) for x in xs]).astype(BF16)

    lse_b = after(lse, *sends)
    if paired:
        dq_far, (d4, d3) = backward_far(0, 2, lse_b, [])
        r3 = shift(d3, swap)
        dq_far, (d2, d1) = backward_far(2, 4, lse_b, [dq_far])
        none = jnp.zeros_like(r3)
        sum4 = plus(d4, jnp.where(odd, r3, none))
        b2 = shift(sum4, hop_back)
        r1 = shift(d1, swap)
    else:
        dq_far, far = backward_far(0, back, lse_b, [])

    for c in range(colors):
        color[c].two = after(color[c].two, dq_far)
    sends = []
    for c in range(colors):
        for axis in orders[c][1:]:
            sends.append(color[c].pick(axis, 1))
            color[c] = color[c].step(axis, move(sends[-1], axis))

    dq_near = after(dq_far, *sends)
    near_kb = max(kb // 2, 8)
    q_grad, own = pl.pallas_call(
        functools.partial(near_kernel, near_kb),
        grid=(tok // qb,),
        out_shape=(sds((tok, width), BF16), sds((tok, 2 * HEAD), F32)),
        in_specs=[SMEM_SPEC, tok_spec, tok_spec, tok_spec, lse_spec, dq_spec, VMEM_SPEC, table_spec, table_spec],
        out_specs=(tok_spec, pl.BlockSpec((tok, 2 * HEAD), lambda i: (0, 0))),
        scratch_shapes=[pltpu.VMEM((tok, HEAD), F32), pltpu.VMEM((tok, HEAD), F32)],
        compiler_params=params(20, "arbitrary"),
        cost_estimate=cost(8 * heads * tok * tok * HEAD, 4 << 20, heads * tok * tok),
        name="near",
    )(doc_lengths, q_rot, d_out, attn, lse, dq_near, kv_home, cos, sin)

    left = color[0].left
    join = len(left)
    one = jnp.concatenate([color[c].one for c in range(colors)], axis=join)
    two = jnp.concatenate([color[c].two for c in range(colors)], axis=join)
    both = Parts(one, two, left)
    for axis in ctx_axes[1:]:
        send = after(both.pick(axis, 1), own)
        recv, lines = move_with_lse(send, axis, lines)
        both = both.step(axis, recv)
    wgrad = both.one.astype(F32) + both.two.astype(F32)

    if paired:
        sum2 = plus(d2, b2, jnp.where(odd, r1, r3))
        arrived = [shift(after(sum2, own), hop_back), jnp.where(odd, none, r1)]
    else:
        arrived = [
            shift(far[back - s], [(i + s, i) for i in range(n_ctx - s)]) for s in range(1, back + 1)
        ]
    k_grad, v_grad = pl.pallas_call(
        functools.partial(home_kernel, len(arrived)),
        out_shape=(sds((tok, HEAD), BF16), sds((tok, HEAD), BF16)),
        in_specs=[VMEM_SPEC] * (3 + len(arrived)),
        out_specs=(VMEM_SPEC, VMEM_SPEC),
        compiler_params=params(4),
        cost_estimate=cost(1 << 20, 2 << 20),
        name="home",
    )(own, cos, sin, *arrived)

    owner_lse = pl.pallas_call(
        owner_kernel,
        out_shape=sds((tok, heads), F32),
        in_specs=[SMEM_SPEC, VMEM_SPEC],
        out_specs=VMEM_SPEC,
        compiler_params=params(4),
        cost_estimate=cost(1 << 18, 1 << 18),
        name="owned",
    )(owner[0], lines.reshape(n_ctx, tok // qb, pack_rows, HEAD))

    return (attn[None], q_grad[None], k_grad[None], v_grad[None], wgrad, owner_lse[None, None])


def solution(mesh):
    in_specs = (
        P("dp", "ctx", None),
        P("dp", "ctx", None),
        P("dp", "ctx", None),
        P("dp", None),
        P("dp", None),
        P(),
        P("dp", "ctx", None),
    )
    out_specs = (
        P("dp", "ctx", None),
        P("dp", "ctx", None),
        P("dp", "ctx", None),
        P("dp", "ctx", None),
        P(None, ("dp", "ctx")),
        P("dp", "ctx", None, None),
    )
    return jax.shard_map(
        on_device, mesh=mesh, in_specs=in_specs, out_specs=out_specs, check_vma=False
    )
```

```python
import functools
import math

import numpy as np

import jax
import jax.numpy as jnp
from jax import lax
from jax.experimental import pallas as pl
from jax.experimental.pallas import tpu as pltpu
from jax.sharding import PartitionSpec as P


HEAD = 128
WIN = 4096
NEG = -1e30
LOG2E = math.log2(math.e)
LN2 = math.log(2.0)
SCALE = 1.0 / math.sqrt(HEAD)
FWD_MIB, WO_MIB, FAR_MIB, NEAR_MIB = 16, 14, 20, 14
F32 = jnp.float32
BF16 = jnp.bfloat16


def doc_starts(lens_ref, pos):
    begin = jnp.int32(0)
    found = jnp.zeros_like(pos)
    for d in range(lens_ref.shape[1]):
        found = jnp.where(pos >= begin, begin, found)
        begin = begin + lens_ref[0, d]
    return found


def sincos(angle):
    turns = jnp.floor(angle * (2.0 / math.pi) + 0.5)
    rest = angle - turns * 1.5703125
    rest = rest - turns * 4.83751296997070312e-4
    rest = rest - turns * 7.54978995489188216e-8
    square = rest * rest
    sine = rest + rest * square * (
        -1.6666654611e-1 + square * (8.3321608736e-3 + square * -1.9515295891e-4)
    )
    cosine = (
        1.0
        - 0.5 * square
        + square
        * square
        * (4.166664568298827e-2 + square * (-1.388731625493765e-3 + square * 2.443315711809948e-5))
    )
    quarter = turns.astype(jnp.int32) & 3
    odd = (quarter & 1) == 1
    out_sin = jnp.where(odd, cosine, sine)
    out_cos = jnp.where(odd, sine, cosine)
    out_sin = jnp.where(quarter >= 2, -out_sin, out_sin)
    out_cos = jnp.where((quarter == 1) | (quarter == 2), -out_cos, out_cos)
    return out_sin, out_cos


def place():
    return lax.axis_index("ctx").astype(jnp.int32), lax.axis_size("ctx")


def rotate(x, cosine, sine):
    return x * cosine + pltpu.roll(x, HEAD // 2, 1) * sine


def prep_kernel(lens_ref, freq_ref, k_ref, v_ref, kv_ref, cos_ref, sin_ref):
    rows = k_ref.shape[0]
    dev, _ = place()
    pos = dev * rows + lax.broadcasted_iota(jnp.int32, (rows, HEAD), 0)
    rel = pos - doc_starts(lens_ref, pos)
    sine, cosine = sincos(rel.astype(F32) * freq_ref[...])
    lane = lax.broadcasted_iota(jnp.int32, (rows, HEAD), 1)
    sine = jnp.where(lane < HEAD // 2, -sine, sine)
    cos_ref[...] = cosine
    sin_ref[...] = sine
    kv_ref[:, :HEAD] = rotate(k_ref[...].astype(F32), cosine, sine).astype(BF16)
    kv_ref[:, HEAD:] = v_ref[...]


def rotq_kernel(q_ref, cos_ref, sin_ref, out_ref):
    for h in range(q_ref.shape[1] // HEAD):
        q = q_ref[:, h * HEAD : (h + 1) * HEAD].astype(F32)
        out_ref[:, h * HEAD : (h + 1) * HEAD] = rotate(q, cos_ref[...], sin_ref[...]).astype(BF16)


def is_paired(n_ctx, back):
    return n_ctx == 8 and back == 4


def slot_list(dev, n_ctx, back):
    if is_paired(n_ctx, back):
        odd = dev % 2 == 1
        skip = jnp.int32(-1)
        return [4, 2, jnp.where(odd, 3, skip), 0, jnp.where(odd, 1, 3), jnp.where(odd, skip, 1)]
    return [back - s for s in range(back + 1)]


def load_slots(slots, refs, scratch, sem, rows, lo=0):
    hi = lo + scratch.shape[0] // rows
    for start in (True, False):
        for i, (slot, ref) in enumerate(zip(slots, refs)):
            if isinstance(slot, int) and not lo <= slot < hi:
                continue

            def move(slot=slot, ref=ref, i=i):
                at = (slot - lo) * rows
                if not isinstance(at, int):
                    at = pl.multiple_of(at, rows)
                copy = pltpu.make_async_copy(ref, scratch.at[pl.ds(at, rows)], sem.at[i])
                if start:
                    copy.start()
                else:
                    copy.wait()

            if isinstance(slot, int):
                move()
            else:
                pl.when((slot >= lo) & (slot < hi))(move)


def tile_ranges(lens_ref, first, qb, kb, base, n_tiles):
    last = first + qb - 1
    low_first = jnp.maximum(doc_starts(lens_ref, first), first - WIN + 1)
    low_last = jnp.maximum(doc_starts(lens_ref, last), last - WIN + 1)
    hi = jnp.minimum((last - base) // kb + 1, n_tiles)
    lo = jnp.minimum(jnp.maximum(low_first - base, 0) // kb, hi)
    full_lo = jnp.clip((jnp.maximum(low_last - base, 0) + kb - 1) // kb, lo, hi)
    full_hi = jnp.clip((first - base + 1) // kb, full_lo, hi)
    return lo, full_lo, full_hi, hi


def over_tiles(ranges, visit, carry):
    lo, full_lo, full_hi, hi = ranges
    carry = lax.fori_loop(full_lo, full_hi, functools.partial(visit, False), carry)

    def edge(i, c):
        return visit(True, jnp.where(lo + i < full_lo, lo + i, full_hi + i - (full_lo - lo)), c)

    return lax.fori_loop(0, (full_lo - lo) + (hi - full_hi), edge, carry)


def fold(x, op):
    return op(x.reshape(x.shape[0] // 8, 8, x.shape[1]), axis=0)


def stack_heads(ref):
    heads = ref.shape[1] // HEAD
    return jnp.concatenate([ref[:, h * HEAD : (h + 1) * HEAD] for h in range(heads)], axis=0)


def query_bounds(lens_ref, first, qb, heads):
    pos = first + lax.broadcasted_iota(jnp.int32, (1, qb), 1)
    low = jnp.maximum(doc_starts(lens_ref, pos), pos - WIN + 1)
    return jnp.concatenate([low] * heads, axis=1), jnp.concatenate([pos] * heads, axis=1)


def masked_scores(s, base, at, low, high):
    key = base + at + lax.broadcasted_iota(jnp.int32, (s.shape[0], 1), 0)
    return jnp.where((key >= low) & (key <= high), s, NEG)


NT = (((1,), (1,)), ((), ()))
NN = (((1,), (0,)), ((), ()))
TN = (((0,), (0,)), ((), ()))


def dot(a, b, dims):
    return lax.dot_general(a, b, dims, preferred_element_type=F32)


def fwd_kernel(n_refs, back, kb, lens_ref, q_ref, *rest):
    kv_refs = rest[:n_refs]
    o_ref, keep_ref, lse_ref, pack_ref, kv_scr, sem = rest[n_refs:]
    step = pl.program_id(0)
    qb, width = q_ref.shape
    heads = width // HEAD
    rows = heads * qb
    tok = kv_refs[0].shape[0]
    dev, n_ctx = place()

    @pl.when(step == 0)
    def _():
        load_slots(slot_list(dev, n_ctx, back), kv_refs, kv_scr, sem, tok)

    base = (dev - back) * tok
    first = dev * tok + step * qb
    q = stack_heads(q_ref)
    low, high = query_bounds(lens_ref, first, qb, heads)
    factor = SCALE * LOG2E

    def visit(masked, j, carry):
        top, total, acc = carry
        at = pl.multiple_of(j * kb, kb)
        s = dot(kv_scr[pl.ds(at, kb), :HEAD], q, NT)
        if masked:
            s = masked_scores(s, base, at, low, high)
        new = jnp.maximum(top, jnp.max(fold(s, jnp.max), axis=0, keepdims=True) * factor)
        alpha = jnp.exp2(top - new)
        p = jnp.exp2(s * factor - new)
        total = total * alpha + fold(p, jnp.sum)
        acc = acc * alpha + dot(kv_scr[pl.ds(at, kb), HEAD:], p.astype(BF16), TN)
        return new, total, acc

    carry = (jnp.full((1, rows), NEG, F32), jnp.zeros((8, rows), F32), jnp.zeros((HEAD, rows), F32))
    ranges = tile_ranges(lens_ref, first, qb, kb, base, kv_scr.shape[0] // kb)
    top, total, acc = over_tiles(ranges, visit, carry)
    total = jnp.sum(total, axis=0, keepdims=True)
    lse = (top + jnp.log2(total)) * LN2
    out = acc / total
    for h in range(heads):
        lse_ref[h : h + 1, :] = lse[:, h * qb : (h + 1) * qb]
        part = jnp.transpose(out[:, h * qb : (h + 1) * qb]).astype(BF16)
        o_ref[:, h * HEAD : (h + 1) * HEAD] = part
        keep_ref[:, h * HEAD : (h + 1) * HEAD] = part
    lines = jnp.concatenate(
        [lse[:, c * HEAD : (c + 1) * HEAD] for c in range(rows // HEAD)], axis=0
    )
    coarse = lines.astype(BF16)
    fine = (lines - coarse.astype(F32)).astype(BF16)
    pack_ref[0] = jnp.concatenate([coarse, fine], axis=0)


def delta_of(dy_ref, o_ref):
    prod = stack_heads(dy_ref).astype(F32) * stack_heads(o_ref).astype(F32)
    qb = dy_ref.shape[0]
    return [
        jnp.sum(jnp.transpose(prod[i : i + qb]), axis=0, keepdims=True)
        for i in range(0, prod.shape[0], qb)
    ]


def bwd_core(lens_ref, q_ref, dy_ref, delta_ref, lse_ref, kv, base, kb, dk_scr, dv_scr, dq):
    qb, width = q_ref.shape
    heads = width // HEAD
    tok = qb * pl.num_programs(0)
    dev, _ = place()
    first = dev * tok + pl.program_id(0) * qb
    q, dy = stack_heads(q_ref), stack_heads(dy_ref)
    lse = jnp.concatenate([lse_ref[h : h + 1, :] for h in range(heads)], axis=1) * LOG2E
    delta = jnp.concatenate([delta_ref[h : h + 1, :] for h in range(heads)], axis=1)
    low, high = query_bounds(lens_ref, first, qb, heads)
    factor = SCALE * LOG2E

    def visit(masked, j, dq):
        at = pl.multiple_of(j * kb, kb)
        k, v = kv[pl.ds(at, kb), :HEAD], kv[pl.ds(at, kb), HEAD:]
        s = dot(k, q, NT)
        if masked:
            s = masked_scores(s, base, at, low, high)
        p = jnp.exp2(s * factor - lse)
        ds = (p * (dot(v, dy, NT) - delta)).astype(BF16)
        dv_scr[pl.ds(at, kb), :] += dot(p.astype(BF16), dy, NN)
        dk_scr[pl.ds(at, kb), :] += dot(ds, q, NN)
        return dq + dot(k, ds, TN)

    return over_tiles(tile_ranges(lens_ref, first, qb, kb, base, kv.shape[0] // kb), visit, dq)


def far_kernel(n_refs, back, lo, has_dq, kb, lens_ref, q_ref, dy_ref, o_ref, lse_ref, *rest):
    kv_refs = rest[:n_refs]
    dqin_ref = rest[n_refs] if has_dq else None
    dq_ref, far_ref, *rest = rest[n_refs + has_dq :]
    if has_dq:
        delta_ref = o_ref
    else:
        delta_ref, *rest = rest
        for h, line in enumerate(delta_of(dy_ref, o_ref)):
            delta_ref[h : h + 1, :] = line
    kv_scr, dk_scr, dv_scr, sem = rest
    tok = kv_refs[0].shape[0]
    dev, n_ctx = place()
    step = pl.program_id(0)

    @pl.when(step == 0)
    def _():
        load_slots(slot_list(dev, n_ctx, back)[1:], kv_refs, kv_scr, sem, tok, lo)
        dk_scr[...] = jnp.zeros_like(dk_scr)
        dv_scr[...] = jnp.zeros_like(dv_scr)

    base = (dev - back + lo) * tok
    dq = dqin_ref[0] if has_dq else jnp.zeros(dq_ref.shape[1:], F32)
    dq_ref[0] = bwd_core(
        lens_ref, q_ref, dy_ref, delta_ref, lse_ref, kv_scr, base, kb, dk_scr, dv_scr, dq
    )

    @pl.when(step == pl.num_programs(0) - 1)
    def _():
        for r in range(far_ref.shape[0]):
            far_ref[r, :, :HEAD] = dk_scr[r * tok : (r + 1) * tok, :].astype(BF16)
            far_ref[r, :, HEAD:] = dv_scr[r * tok : (r + 1) * tok, :].astype(BF16)


def near_kernel(kb, lens_ref, q_ref, dy_ref, delta_ref, lse_ref, dqin_ref, kv_ref, cos_ref, sin_ref,
                dq_ref, own_ref, dk_scr, dv_scr):
    tok = kv_ref.shape[0]
    dev, _ = place()
    step = pl.program_id(0)
    qb = q_ref.shape[0]

    @pl.when(step == 0)
    def _():
        dk_scr[...] = jnp.zeros_like(dk_scr)
        dv_scr[...] = jnp.zeros_like(dv_scr)

    dq = bwd_core(
        lens_ref, q_ref, dy_ref, delta_ref, lse_ref, kv_ref, dev * tok, kb, dk_scr, dv_scr, dqin_ref[0]
    )
    for h in range(q_ref.shape[1] // HEAD):
        part = jnp.transpose(dq[:, h * qb : (h + 1) * qb]) * SCALE
        dq_ref[:, h * HEAD : (h + 1) * HEAD] = rotate(part, cos_ref[...], -sin_ref[...]).astype(BF16)

    @pl.when(step == pl.num_programs(0) - 1)
    def _():
        own_ref[:, :HEAD] = dk_scr[...]
        own_ref[:, HEAD:] = dv_scr[...]


def wo_kernel(core, a_ref, g_ref, *rest):
    g_scr, sem = rest[-2:]
    outs, other_ref = rest[:4], (rest[4] if core else None)
    dev, n_ctx = place()
    dp = lax.axis_index("dp").astype(jnp.int32)
    _, wide = g_scr.shape[1:]
    n_half = g_scr.shape[0]
    col = wide // n_ctx
    rows = outs[0].shape[1]

    def fetch(i, to, bit, dst, where):
        start = (((2 * i + bit) ^ dp) * n_ctx + (to ^ dev)) * col
        src = g_ref.at[:, pl.ds(pl.multiple_of(start, col), col)]
        return pltpu.make_async_copy(src, dst.at[i, :, pl.ds(to * col, col)], sem.at[where, i * n_ctx + to])

    def each(what, *args):
        for i in range(n_half):
            for to in range(n_ctx):
                getattr(fetch(i, to, *args), what)()

    if core:
        each("start", 1, g_scr, 0)
        each("start", 0, other_ref, 1)
    at = jnp.transpose(a_ref[...])
    for i in range(n_half):
        if core:
            for to in range(n_ctx):
                fetch(i, to, 1, g_scr, 0).wait()
        block = g_scr[i] if core else g_ref[i]
        res = jnp.dot(at, block, preferred_element_type=F32).astype(BF16)
        for to in range(n_ctx):
            part = res[:, to * col : (to + 1) * col]
            outs[i & 1][(i >> 1) * n_ctx + to] = part[:rows]
            outs[2 + ((to >> 1) & 1)][i * (n_ctx // 2) + ((to >> 2) << 1 | (to & 1))] = part[rows:]
    if core:
        each("wait", 0, other_ref, 1)


def home_kernel(n_in, own_ref, cos_ref, sin_ref, *rest):
    ins, (dk_ref, dv_ref) = rest[:n_in], rest[n_in:]
    total = own_ref[...]
    for ref in ins:
        total = total + ref[...].astype(F32)
    dk_ref[...] = rotate(total[:, :HEAD] * SCALE, cos_ref[...], -sin_ref[...]).astype(BF16)
    dv_ref[...] = total[:, HEAD:].astype(BF16)


def final_kernel(bits, owner_ref, one_ref, recv_ref, lse_ref, wgrad_ref, out_ref, all_scr):
    size = one_ref.shape[0]
    wgrad_ref[...] = one_ref[...].astype(F32) + recv_ref[:size].astype(F32)
    dev, n_ctx = place()
    heads, tok = out_ref.shape
    block_len = tok // n_ctx
    count = lse_ref.shape[0]
    all_scr[:count] = lse_ref[...].astype(F32)
    all_scr[count:] = recv_ref[size:].astype(F32)
    each = 2 * count // n_ctx
    chunks = tok // 2 // HEAD
    of_half = heads * chunks
    for c in range(n_ctx):
        away = dev ^ c
        index = jnp.int32(0)
        for k, b in enumerate(bits):
            index = index | (((away >> b) & 1) << k)
        raw = all_scr[pl.ds(pl.multiple_of(index * each, each), each), :]
        mine = jnp.zeros((heads, block_len), F32)
        for s in range(n_ctx):
            half, rest = divmod(s * block_len, tok // 2)
            chunk, lane = divmod(rest, HEAD)
            parts = []
            for h in range(heads):
                row = half * 2 * of_half + h * chunks + chunk
                line = raw[row : row + 1] + raw[row + of_half : row + of_half + 1]
                parts.append(line[:, lane : lane + block_len])
            mine = jnp.where(owner_ref[c * n_ctx + s] == dev, jnp.concatenate(parts, axis=0), mine)
        out_ref[:, c * block_len : (c + 1) * block_len] = mine


SMEM_SPEC = pl.BlockSpec(memory_space=pltpu.SMEM)
VMEM_SPEC = pl.BlockSpec(memory_space=pltpu.VMEM)
ANY_SPEC = pl.BlockSpec(memory_space=pl.ANY)


def params(mib, *semantics):
    return pltpu.CompilerParams(dimension_semantics=semantics or None, vmem_limit_bytes=mib << 20)


def cost(flops, size, exps=0):
    return pl.CostEstimate(flops=int(flops), bytes_accessed=int(size), transcendentals=int(exps))


def after(x, *others):
    return lax.optimization_barrier((x, *others))[0]


def on_device(queries, keys, values, doc_lengths, owner, out_weight, out_grad):
    n_ctx = lax.axis_size("ctx")
    n_dp = lax.axis_size("dp")
    dev = lax.axis_index("ctx").astype(jnp.int32)
    dp = lax.axis_index("dp").astype(jnp.int32)
    tok = queries.shape[1]
    width = queries.shape[2]
    heads = width // HEAD
    seq_len = tok * n_ctx
    d_model = out_grad.shape[2]
    reach = min(WIN, seq_len // 2)
    back = min(-(-reach // tok), n_ctx - 1)
    sds = jax.ShapeDtypeStruct

    half = HEAD // 2
    freq = (10000.0 ** (-2.0 * np.arange(half) / HEAD)).astype(np.float32)
    freq = jnp.asarray(np.concatenate([freq, freq])[None, :])

    def shift(x, pairs):
        return lax.ppermute(x, "ctx", pairs)

    hop = [(i, i + 2) for i in range(n_ctx - 2)]
    hop_back = [(b, a) for a, b in hop]
    up = [(i, i + 1) for i in range(0, n_ctx, 2)]
    down = [(b, a) for a, b in up]
    swap = up + down
    odd = dev % 2 == 1
    paired = is_paired(n_ctx, back)

    kv_home, cos, sin = pl.pallas_call(
        prep_kernel,
        out_shape=(sds((tok, 2 * HEAD), BF16), sds((tok, HEAD), F32), sds((tok, HEAD), F32)),
        in_specs=[SMEM_SPEC] + [VMEM_SPEC] * 3,
        out_specs=(VMEM_SPEC,) * 3,
        compiler_params=params(58),
        cost_estimate=cost(1 << 22, 1 << 20),
        name="prep",
    )(doc_lengths, freq, keys[0], values[0])

    def d_out_of(grad):
        return lax.dot_general(
            grad, out_weight, (((1,), (1,)), ((), ())), preferred_element_type=F32
        ).astype(BF16)

    def rotated_queries(x):
        return pl.pallas_call(
            rotq_kernel,
            out_shape=sds((tok, width), BF16),
            in_specs=[VMEM_SPEC] * 3,
            out_specs=VMEM_SPEC,
            compiler_params=params(4),
            cost_estimate=cost(1 << 22, 2 << 20),
            name="rotq",
        )(x, cos, sin)

    if paired:
        a1 = shift(kv_home, hop)
        e1 = shift(kv_home, up)
        q_rot = rotated_queries(queries[0])
        s1 = shift(a1, swap)
        a2 = shift(a1, hop)
        o3 = shift(a2, down)
        d_out = d_out_of(after(out_grad[0], a2))
        blocks = [kv_home, a1, e1, a2, s1, o3]
    else:
        blocks = [kv_home] + [
            shift(kv_home, [(i, i + s) for i in range(n_ctx - s)]) for s in range(1, back + 1)
        ]
        q_rot = rotated_queries(queries[0])
        d_out = d_out_of(out_grad[0])

    n_keys = (back + 1) * tok
    qb = tok // 2
    kb = tok
    tok_spec = pl.BlockSpec((qb, width), lambda i: (i, 0))
    lse_spec = pl.BlockSpec((heads, qb), lambda i: (0, i))
    table_spec = pl.BlockSpec((qb, HEAD), lambda i: (i, 0))
    dq_spec = pl.BlockSpec((1, HEAD, heads * qb), lambda i: (i, 0, 0))
    pairs = heads * tok * (tok + reach) // 2
    pack_rows = 2 * heads * qb // HEAD
    attn_out, attn, lse, pack = pl.pallas_call(
        functools.partial(fwd_kernel, len(blocks), back, kb),
        grid=(tok // qb,),
        out_shape=(
            sds((tok, width), BF16),
            sds((tok, width), BF16),
            sds((heads, tok), F32),
            sds((tok // qb, pack_rows, HEAD), BF16),
        ),
        in_specs=[SMEM_SPEC, tok_spec] + [ANY_SPEC] * len(blocks),
        out_specs=(tok_spec, tok_spec, lse_spec, pl.BlockSpec((1, pack_rows, HEAD), lambda i: (i, 0, 0))),
        scratch_shapes=[
            pltpu.VMEM((n_keys, 2 * HEAD), BF16),
            pltpu.SemaphoreType.DMA((len(blocks),)),
        ],
        compiler_params=params(FWD_MIB, "arbitrary"),
        cost_estimate=cost(4 * pairs * HEAD, 4 << 20, pairs),
        name="fwd",
    )(doc_lengths, q_rot, *blocks)

    col = d_model // (n_dp * n_ctx)
    bits_dp = n_dp.bit_length() - 1
    bits_ctx = n_ctx.bit_length() - 1
    rows = width // 2
    n_half = n_dp // 2
    wide = n_ctx * col

    def shapes_of(sizes):
        return [sds((size, rows, col), BF16) for size in sizes]

    sizes = [n_half // 2 * n_ctx] * 2 + [n_half * n_ctx // 2] * 2

    def partial_wo(core, grads):
        return pl.pallas_call(
            functools.partial(wo_kernel, core),
            out_shape=shapes_of(sizes) + ([sds((n_half, tok, wide), BF16)] if core else []),
            in_specs=[VMEM_SPEC, ANY_SPEC if core else VMEM_SPEC],
            out_specs=[VMEM_SPEC] * (4 + core),
            scratch_shapes=[
                pltpu.VMEM((n_half, tok, wide), BF16),
                pltpu.SemaphoreType.DMA((2, n_half * n_ctx)),
            ],
            compiler_params=params(WO_MIB),
            cost_estimate=cost(tok * width * d_model, 6 << 20),
        )(attn, grads)

    def partial_wo_narrow(core):
        grads = out_grad[0].reshape(tok, n_dp, n_ctx, col)
        grads = jnp.take(grads, (2 * jnp.arange(n_half) + core) ^ dp, axis=1)
        grads = jnp.take(grads, jnp.arange(n_ctx) ^ dev, axis=2)
        res = jnp.einsum("tr,tabc->abrc", attn, grads, preferred_element_type=F32).astype(BF16)
        upper = res[:, :, :rows].reshape(n_half // 2, 2, n_ctx, rows, col)
        lower = res[:, :, rows:].reshape(n_half, n_ctx // 4, 2, 2, rows, col)
        outs = [upper[:, w].reshape(-1, rows, col) for w in range(2)]
        return outs + [lower[:, :, w].reshape(-1, rows, col) for w in range(2)]

    def exchange(x, axis, bit, size):
        return lax.ppermute(x, axis, [(i, i ^ bit) for i in range(size)])

    size_of = {"dp": n_dp, "ctx": n_ctx}
    lead = [("dp", b) for b in range(bits_dp - 1, 0, -1)]
    lead += [("ctx", b) for b in range(bits_ctx - 1, -1, -1)]

    def move(x, axis):
        return exchange(x, axis[0], 1 << axis[1], size_of[axis[0]])

    class Parts:
        def __init__(self, addends, left):
            self.left = list(left)
            self.addends = [x.reshape((2,) * len(self.left) + x.shape[-2:]) for x in addends]

        def pick(self, axis, which):
            at = self.left.index(axis)
            picked = [lax.index_in_dim(x, which, at, keepdims=False) for x in self.addends]
            return functools.reduce(jnp.add, [x.astype(F32) for x in picked]).astype(BF16)

        def step(self, axis, recv):
            at = self.left.index(axis)
            kept = [lax.index_in_dim(x, 0, at, keepdims=False) for x in self.addends]
            return Parts(kept + [recv], [a for a in self.left if a != axis])

    firsts = [("dp", 1), ("ctx", 1)]
    if col % HEAD == 0:
        *wo_send, grads_keep = partial_wo(1, out_grad[0])
        wo_recv = [None] * 4
        for n in (1, 3, 0, 2):
            wo_recv[n] = exchange(wo_send[n], "dp", 1, n_dp)
        wo_keep = partial_wo(0, grads_keep)
    else:
        wo_recv = [exchange(x, "dp", 1, n_dp) for x in partial_wo_narrow(1)]
        wo_keep = partial_wo_narrow(0)
    lefts = [[a for a in lead if a != firsts[c]] for c in range(2)]
    sends = []
    color = []
    for c in range(2):
        kept, sent = [Parts([wo_keep[2 * c + w], wo_recv[2 * c + w]], lefts[c]) for w in range(2)]
        color.append(kept)
        total = functools.reduce(jnp.add, [x.astype(F32) for x in sent.addends]).astype(BF16)
        sends.append(total)

    lines = pack.reshape(-1, col)

    def with_lse(x, lse_of):
        return jnp.concatenate([x.reshape(-1, col), lse_of], axis=0)

    recv = move(sends[0], firsts[0])
    color[0] = Parts(color[0].addends + [recv], lefts[0])
    size = sends[1].size // col
    recv = move(with_lse(sends[1], lines), firsts[1])
    color[1] = Parts(color[1].addends + [recv[:size].reshape(sends[1].shape)], lefts[1])
    lines = jnp.concatenate([lines, recv[size:]], axis=0)

    def backward_far(lo, hi, lse_in, third, dq_in):
        count = hi - lo
        new = [] if dq_in else [(sds((heads, tok), F32), lse_spec)]
        return pl.pallas_call(
            functools.partial(far_kernel, len(blocks) - 1, back, lo, len(dq_in), kb),
            grid=(tok // qb,),
            out_shape=[sds((tok // qb, HEAD, heads * qb), F32), sds((count, tok, 2 * HEAD), BF16)]
            + [n[0] for n in new],
            in_specs=[SMEM_SPEC, tok_spec, tok_spec, lse_spec if dq_in else tok_spec, lse_spec]
            + [ANY_SPEC] * (len(blocks) - 1)
            + [dq_spec] * len(dq_in),
            out_specs=[dq_spec, pl.BlockSpec((count, tok, 2 * HEAD), lambda i: (0, 0, 0))]
            + [n[1] for n in new],
            scratch_shapes=[
                pltpu.VMEM((count * tok, 2 * HEAD), BF16),
                pltpu.VMEM((count * tok, HEAD), F32),
                pltpu.VMEM((count * tok, HEAD), F32),
                pltpu.SemaphoreType.DMA((len(blocks) - 1,)),
            ],
            compiler_params=params(FAR_MIB, "arbitrary"),
            cost_estimate=cost(8 * pairs * HEAD, 8 << 20, pairs),
        )(doc_lengths, q_rot, d_out, third, lse_in, *blocks[1:], *dq_in)

    def plus(*xs):
        return functools.reduce(jnp.add, [x.astype(F32) for x in xs]).astype(BF16)

    lse_b = after(lse, *sends)
    if paired:
        dq_far, (d4, d3), delta = backward_far(0, 2, lse_b, attn, [])
        r3 = shift(d3, swap)
        dq_far, (d2, d1) = backward_far(2, 4, lse_b, delta, [dq_far])
        none = jnp.zeros_like(r3)
        sum4 = plus(d4, jnp.where(odd, r3, none))
        b2 = shift(sum4, hop_back)
        r1 = shift(d1, swap)
    else:
        dq_far, far, delta = backward_far(0, back, lse_b, attn, [])

    seconds = [firsts[1], firsts[0]]
    extra = [a for a in lead if a[0] == "dp" and a not in firsts]
    sends = []
    for c in range(2):
        color[c].addends[-1] = after(color[c].addends[-1], dq_far)
        for axis in [seconds[c]] + extra:
            sends.append(color[c].pick(axis, 1))
            color[c] = color[c].step(axis, move(sends[-1], axis))

    dq_near = after(dq_far, *sends)
    near_kb = max(kb // 2, 8)
    q_grad, own = pl.pallas_call(
        functools.partial(near_kernel, near_kb),
        grid=(tok // qb,),
        out_shape=(sds((tok, width), BF16), sds((tok, 2 * HEAD), F32)),
        in_specs=[SMEM_SPEC, tok_spec, tok_spec, lse_spec, lse_spec, dq_spec, VMEM_SPEC, table_spec, table_spec],
        out_specs=(tok_spec, pl.BlockSpec((tok, 2 * HEAD), lambda i: (0, 0))),
        scratch_shapes=[pltpu.VMEM((tok, HEAD), F32), pltpu.VMEM((tok, HEAD), F32)],
        compiler_params=params(NEAR_MIB, "arbitrary"),
        cost_estimate=cost(8 * heads * tok * tok * HEAD, 4 << 20, heads * tok * tok),
        name="near",
    )(doc_lengths, q_rot, d_out, delta, lse, dq_near, kv_home, cos, sin)

    ctx_axes = [("ctx", 0)] + [("ctx", b) for b in range(2, bits_ctx)]
    lse_bits = [1, 0] + list(range(2, bits_ctx))
    both = None
    for axis in ctx_axes:
        if both is None:
            pieces = [jnp.concatenate([color[c].pick(axis, w) for c in range(2)], axis=-2) for w in range(2)]
            left = [a for a in color[0].left if a != axis]
            send = after(pieces[1], own)
            kept = [pieces[0]]
        else:
            send = both.pick(axis, 1)
            left = [a for a in both.left if a != axis]
            at = both.left.index(axis)
            kept = [lax.index_in_dim(x, 0, at, keepdims=False) for x in both.addends]
        size = send.size // col
        recv = move(with_lse(send, lines), axis)
        if axis != ctx_axes[-1]:
            both = Parts(kept + [recv[:size].reshape(send.shape)], left)
            lines = jnp.concatenate([lines, recv[size:]], axis=0)
    last = functools.reduce(jnp.add, [x.astype(F32) for x in kept]).astype(BF16)

    if paired:
        sum2 = plus(d2, b2, jnp.where(odd, r1, r3))
        arrived = [shift(after(sum2, own), hop_back), jnp.where(odd, none, r1)]
    else:
        arrived = [
            shift(far[back - s], [(i + s, i) for i in range(n_ctx - s)]) for s in range(1, back + 1)
        ]
    k_grad, v_grad = pl.pallas_call(
        functools.partial(home_kernel, len(arrived)),
        out_shape=(sds((tok, HEAD), BF16), sds((tok, HEAD), BF16)),
        in_specs=[VMEM_SPEC] * (3 + len(arrived)),
        out_specs=(VMEM_SPEC, VMEM_SPEC),
        compiler_params=params(4),
        cost_estimate=cost(1 << 20, 2 << 20),
        name="home",
    )(own, cos, sin, *arrived)

    if col != HEAD:
        tail_rows = recv[width:].reshape(-1, HEAD)
        recv = jnp.concatenate([jnp.pad(recv[:width], ((0, 0), (0, HEAD - col))), tail_rows], axis=0)
        last = jnp.pad(last, ((0, 0), (0, HEAD - col)))
        lines = lines.reshape(-1, HEAD)
    wgrad, owner_lse = pl.pallas_call(
        functools.partial(final_kernel, lse_bits),
        out_shape=(sds((width, HEAD), F32), sds((heads, tok), F32)),
        in_specs=[SMEM_SPEC] + [VMEM_SPEC] * 3,
        out_specs=(VMEM_SPEC,) * 2,
        scratch_shapes=[pltpu.VMEM((2 * lines.size // HEAD, HEAD), F32)],
        compiler_params=params(8),
        cost_estimate=cost(1 << 18, 1 << 20),
        name="final",
    )(owner[0], last, recv, lines)
    wgrad = wgrad[:, :col]
    owner_lse = jnp.transpose(owner_lse)

    return (attn_out[None], q_grad[None], k_grad[None], v_grad[None], wgrad, owner_lse[None, None])


def solution(mesh):
    in_specs = (
        P("dp", "ctx", None),
        P("dp", "ctx", None),
        P("dp", "ctx", None),
        P("dp", None),
        P("dp", None),
        P(),
        P("dp", "ctx", None),
    )
    out_specs = (
        P("dp", "ctx", None),
        P("dp", "ctx", None),
        P("dp", "ctx", None),
        P("dp", "ctx", None),
        P(None, ("dp", "ctx")),
        P("dp", "ctx", None, None),
    )

    return jax.shard_map(
        on_device, mesh=mesh, in_specs=in_specs, out_specs=out_specs, check_vma=False
    )
```

```python
import functools
import math

import numpy as np

import jax
import jax.numpy as jnp
from jax import lax
from jax.experimental import pallas as pl
from jax.experimental.pallas import tpu as pltpu
from jax.sharding import PartitionSpec as P


HEAD = 128
WIN = 4096
NEG = -1e30
LOG2E = math.log2(math.e)
LN2 = math.log(2.0)
SCALE = 1.0 / math.sqrt(HEAD)
FWD_MIB, WO_MIB, FAR_MIB, NEAR_MIB = 16, 14, 20, 14
F32 = jnp.float32
BF16 = jnp.bfloat16


def doc_starts(lens_ref, pos):
    begin = jnp.int32(0)
    found = jnp.zeros_like(pos)
    for d in range(lens_ref.shape[1]):
        found = jnp.where(pos >= begin, begin, found)
        begin = begin + lens_ref[0, d]
    return found


def sincos(angle):
    turns = jnp.floor(angle * (2.0 / math.pi) + 0.5)
    rest = angle - turns * 1.5703125
    rest = rest - turns * 4.83751296997070312e-4
    rest = rest - turns * 7.54978995489188216e-8
    square = rest * rest
    sine = rest + rest * square * (
        -1.6666654611e-1 + square * (8.3321608736e-3 + square * -1.9515295891e-4)
    )
    cosine = (
        1.0
        - 0.5 * square
        + square
        * square
        * (4.166664568298827e-2 + square * (-1.388731625493765e-3 + square * 2.443315711809948e-5))
    )
    quarter = turns.astype(jnp.int32) & 3
    odd = (quarter & 1) == 1
    out_sin = jnp.where(odd, cosine, sine)
    out_cos = jnp.where(odd, sine, cosine)
    out_sin = jnp.where(quarter >= 2, -out_sin, out_sin)
    out_cos = jnp.where((quarter == 1) | (quarter == 2), -out_cos, out_cos)
    return out_sin, out_cos


def place():
    return lax.axis_index("ctx").astype(jnp.int32), lax.axis_size("ctx")


def rotate(x, cosine, sine):
    return x * cosine + pltpu.roll(x, HEAD // 2, 1) * sine


def prep_kernel(lens_ref, freq_ref, k_ref, v_ref, kv_ref, cos_ref, sin_ref):
    rows = k_ref.shape[0]
    dev, _ = place()
    pos = dev * rows + lax.broadcasted_iota(jnp.int32, (rows, HEAD), 0)
    rel = pos - doc_starts(lens_ref, pos)
    sine, cosine = sincos(rel.astype(F32) * freq_ref[...])
    lane = lax.broadcasted_iota(jnp.int32, (rows, HEAD), 1)
    sine = jnp.where(lane < HEAD // 2, -sine, sine)
    cos_ref[...] = cosine
    sin_ref[...] = sine
    kv_ref[:, :HEAD] = rotate(k_ref[...].astype(F32), cosine, sine).astype(BF16)
    kv_ref[:, HEAD:] = v_ref[...]


def rotq_kernel(q_ref, cos_ref, sin_ref, out_ref):
    for h in range(q_ref.shape[1] // HEAD):
        q = q_ref[:, h * HEAD : (h + 1) * HEAD].astype(F32)
        out_ref[:, h * HEAD : (h + 1) * HEAD] = rotate(q, cos_ref[...], sin_ref[...]).astype(BF16)


def is_paired(n_ctx, back):
    return n_ctx == 8 and back == 4


def slot_list(dev, n_ctx, back):
    if is_paired(n_ctx, back):
        odd = dev % 2 == 1
        skip = jnp.int32(-1)
        return [4, 2, jnp.where(odd, 3, skip), 0, jnp.where(odd, 1, 3), jnp.where(odd, skip, 1)]
    return [back - s for s in range(back + 1)]


def load_slots(slots, refs, scratch, sem, rows, lo=0):
    hi = lo + scratch.shape[0] // rows
    for start in (True, False):
        for i, (slot, ref) in enumerate(zip(slots, refs)):
            if isinstance(slot, int) and not lo <= slot < hi:
                continue

            def move(slot=slot, ref=ref, i=i):
                at = (slot - lo) * rows
                if not isinstance(at, int):
                    at = pl.multiple_of(at, rows)
                copy = pltpu.make_async_copy(ref, scratch.at[pl.ds(at, rows)], sem.at[i])
                if start:
                    copy.start()
                else:
                    copy.wait()

            if isinstance(slot, int):
                move()
            else:
                pl.when((slot >= lo) & (slot < hi))(move)


def tile_ranges(lens_ref, first, qb, kb, base, n_tiles):
    last = first + qb - 1
    low_first = jnp.maximum(doc_starts(lens_ref, first), first - WIN + 1)
    low_last = jnp.maximum(doc_starts(lens_ref, last), last - WIN + 1)
    hi = jnp.minimum((last - base) // kb + 1, n_tiles)
    lo = jnp.minimum(jnp.maximum(low_first - base, 0) // kb, hi)
    full_lo = jnp.clip((jnp.maximum(low_last - base, 0) + kb - 1) // kb, lo, hi)
    full_hi = jnp.clip((first - base + 1) // kb, full_lo, hi)
    return lo, full_lo, full_hi, hi


def over_tiles(ranges, visit, carry):
    lo, full_lo, full_hi, hi = ranges
    carry = lax.fori_loop(full_lo, full_hi, functools.partial(visit, False), carry)

    def edge(i, c):
        return visit(True, jnp.where(lo + i < full_lo, lo + i, full_hi + i - (full_lo - lo)), c)

    return lax.fori_loop(0, (full_lo - lo) + (hi - full_hi), edge, carry)


def fold(x, op):
    return op(x.reshape(x.shape[0] // 8, 8, x.shape[1]), axis=0)


def stack_heads(ref):
    heads = ref.shape[1] // HEAD
    return jnp.concatenate([ref[:, h * HEAD : (h + 1) * HEAD] for h in range(heads)], axis=0)


def query_bounds(lens_ref, first, qb, heads):
    pos = first + lax.broadcasted_iota(jnp.int32, (1, qb), 1)
    low = jnp.maximum(doc_starts(lens_ref, pos), pos - WIN + 1)
    return jnp.concatenate([low] * heads, axis=1), jnp.concatenate([pos] * heads, axis=1)


def masked_scores(s, base, at, low, high):
    key = base + at + lax.broadcasted_iota(jnp.int32, (s.shape[0], 1), 0)
    return jnp.where((key >= low) & (key <= high), s, NEG)


NT = (((1,), (1,)), ((), ()))
NN = (((1,), (0,)), ((), ()))
TN = (((0,), (0,)), ((), ()))


def dot(a, b, dims):
    return lax.dot_general(a, b, dims, preferred_element_type=F32)


def fwd_kernel(picks, back, resume, finish, lens_ref, q_ref, *rest):
    kv_refs, rest = rest[: len(picks)], rest[len(picks) :]
    if resume:
        acc_in_ref, stat_in_ref, *rest = rest
    *outs, kv_scr, sem = rest
    step = pl.program_id(0)
    qb, width = q_ref.shape
    heads = width // HEAD
    rows = heads * qb
    kb = kv_refs[0].shape[0]
    dev, n_ctx = place()
    slots = [slot_list(dev, n_ctx, back)[p] for p in picks]

    @pl.when(step == 0)
    def _():
        copies = [
            pltpu.make_async_copy(ref, kv_scr.at[i], sem.at[i]) for i, ref in enumerate(kv_refs)
        ]
        for copy in copies:
            copy.start()
        for copy in copies:
            copy.wait()

    base = (dev - back) * kb
    first = dev * kb + step * qb
    q = stack_heads(q_ref)
    low, high = query_bounds(lens_ref, first, qb, heads)
    factor = SCALE * LOG2E
    lo, full_lo, full_hi, hi = tile_ranges(lens_ref, first, qb, kb, base, back + 1)

    def visit(masked, i, slot, carry):
        top, total, acc = carry
        s = dot(kv_scr[i, :, :HEAD], q, NT)
        if masked:
            s = masked_scores(s, base, slot * kb, low, high)
        new = jnp.maximum(top, jnp.max(fold(s, jnp.max), axis=0, keepdims=True) * factor)
        alpha = jnp.exp2(top - new)
        p = jnp.exp2(s * factor - new)
        total = total * alpha + fold(p, jnp.sum)
        acc = acc * alpha + dot(kv_scr[i, :, HEAD:], p.astype(BF16), TN)
        return new, total, acc

    def block(i, carry):
        slot = jnp.int32(slots[0])
        for n in range(1, len(slots)):
            slot = jnp.where(i == n, slots[n], slot)
        seen = (slot >= lo) & (slot < hi)
        full = seen & (slot >= full_lo) & (slot < full_hi)
        for masked, go in ((False, full), (True, seen & ~full)):
            carry = lax.fori_loop(
                0, go.astype(jnp.int32), lambda _, c, masked=masked: visit(masked, i, slot, c), carry
            )
        return carry

    if resume:
        carry = (stat_in_ref[0, 0:1], stat_in_ref[0, 8:16], acc_in_ref[0])
    else:
        carry = (jnp.full((1, rows), NEG, F32), jnp.zeros((8, rows), F32), jnp.zeros((HEAD, rows), F32))
    top, total, acc = lax.fori_loop(0, len(picks), block, carry)
    if not finish:
        acc_ref, stat_ref = outs
        acc_ref[0] = acc
        stat_ref[0, 0:8] = jnp.broadcast_to(top, (8, rows))
        stat_ref[0, 8:16] = total
        return
    o_ref, keep_ref, lse_ref, pack_ref = outs
    total = jnp.sum(total, axis=0, keepdims=True)
    lse = (top + jnp.log2(total)) * LN2
    out = acc / total
    for h in range(heads):
        lse_ref[h : h + 1, :] = lse[:, h * qb : (h + 1) * qb]
        part = jnp.transpose(out[:, h * qb : (h + 1) * qb]).astype(BF16)
        o_ref[:, h * HEAD : (h + 1) * HEAD] = part
        keep_ref[:, h * HEAD : (h + 1) * HEAD] = part
    lines = jnp.concatenate(
        [lse[:, c * HEAD : (c + 1) * HEAD] for c in range(rows // HEAD)], axis=0
    )
    coarse = lines.astype(BF16)
    fine = (lines - coarse.astype(F32)).astype(BF16)
    pack_ref[0] = jnp.concatenate([coarse, fine], axis=0)


def delta_of(dy_ref, o_ref):
    prod = stack_heads(dy_ref).astype(F32) * stack_heads(o_ref).astype(F32)
    qb = dy_ref.shape[0]
    return [
        jnp.sum(jnp.transpose(prod[i : i + qb]), axis=0, keepdims=True)
        for i in range(0, prod.shape[0], qb)
    ]


def bwd_core(lens_ref, q_ref, dy_ref, delta_ref, lse_ref, kv, base, kb, dk_scr, dv_scr, dq):
    qb, width = q_ref.shape
    heads = width // HEAD
    tok = qb * pl.num_programs(0)
    dev, _ = place()
    first = dev * tok + pl.program_id(0) * qb
    q, dy = stack_heads(q_ref), stack_heads(dy_ref)
    lse = jnp.concatenate([lse_ref[h : h + 1, :] for h in range(heads)], axis=1) * LOG2E
    delta = jnp.concatenate([delta_ref[h : h + 1, :] for h in range(heads)], axis=1)
    low, high = query_bounds(lens_ref, first, qb, heads)
    factor = SCALE * LOG2E

    def visit(masked, j, dq):
        at = pl.multiple_of(j * kb, kb)
        k, v = kv[pl.ds(at, kb), :HEAD], kv[pl.ds(at, kb), HEAD:]
        s = dot(k, q, NT)
        if masked:
            s = masked_scores(s, base, at, low, high)
        p = jnp.exp2(s * factor - lse)
        ds = (p * (dot(v, dy, NT) - delta)).astype(BF16)
        dv_scr[pl.ds(at, kb), :] += dot(p.astype(BF16), dy, NN)
        dk_scr[pl.ds(at, kb), :] += dot(ds, q, NN)
        return dq + dot(k, ds, TN)

    return over_tiles(tile_ranges(lens_ref, first, qb, kb, base, kv.shape[0] // kb), visit, dq)


def far_kernel(n_refs, back, lo, has_dq, kb, lens_ref, q_ref, dy_ref, o_ref, lse_ref, *rest):
    kv_refs = rest[:n_refs]
    dqin_ref = rest[n_refs] if has_dq else None
    dq_ref, far_ref, *rest = rest[n_refs + has_dq :]
    if has_dq:
        delta_ref = o_ref
    else:
        delta_ref, *rest = rest
        for h, line in enumerate(delta_of(dy_ref, o_ref)):
            delta_ref[h : h + 1, :] = line
    kv_scr, dk_scr, dv_scr, sem = rest
    tok = kv_refs[0].shape[0]
    dev, n_ctx = place()
    step = pl.program_id(0)

    @pl.when(step == 0)
    def _():
        load_slots(slot_list(dev, n_ctx, back)[1:], kv_refs, kv_scr, sem, tok, lo)
        dk_scr[...] = jnp.zeros_like(dk_scr)
        dv_scr[...] = jnp.zeros_like(dv_scr)

    base = (dev - back + lo) * tok
    dq = dqin_ref[0] if has_dq else jnp.zeros(dq_ref.shape[1:], F32)
    dq_ref[0] = bwd_core(
        lens_ref, q_ref, dy_ref, delta_ref, lse_ref, kv_scr, base, kb, dk_scr, dv_scr, dq
    )

    @pl.when(step == pl.num_programs(0) - 1)
    def _():
        for r in range(far_ref.shape[0]):
            far_ref[r, :, :HEAD] = dk_scr[r * tok : (r + 1) * tok, :].astype(BF16)
            far_ref[r, :, HEAD:] = dv_scr[r * tok : (r + 1) * tok, :].astype(BF16)


def near_kernel(kb, lens_ref, q_ref, dy_ref, delta_ref, lse_ref, dqin_ref, kv_ref, cos_ref, sin_ref,
                dq_ref, own_ref, dk_scr, dv_scr):
    tok = kv_ref.shape[0]
    dev, _ = place()
    step = pl.program_id(0)
    qb = q_ref.shape[0]

    @pl.when(step == 0)
    def _():
        dk_scr[...] = jnp.zeros_like(dk_scr)
        dv_scr[...] = jnp.zeros_like(dv_scr)

    dq = bwd_core(
        lens_ref, q_ref, dy_ref, delta_ref, lse_ref, kv_ref, dev * tok, kb, dk_scr, dv_scr, dqin_ref[0]
    )
    for h in range(q_ref.shape[1] // HEAD):
        part = jnp.transpose(dq[:, h * qb : (h + 1) * qb]) * SCALE
        dq_ref[:, h * HEAD : (h + 1) * HEAD] = rotate(part, cos_ref[...], -sin_ref[...]).astype(BF16)

    @pl.when(step == pl.num_programs(0) - 1)
    def _():
        own_ref[:, :HEAD] = dk_scr[...]
        own_ref[:, HEAD:] = dv_scr[...]


def wo_kernel(core, a_ref, g_ref, *rest):
    g_scr, sem = rest[-2:]
    outs, other_ref = rest[:4], (rest[4] if core else None)
    dev, n_ctx = place()
    dp = lax.axis_index("dp").astype(jnp.int32)
    _, wide = g_scr.shape[1:]
    n_half = g_scr.shape[0]
    col = wide // n_ctx
    rows = outs[0].shape[1]

    def fetch(i, to, bit, dst, where):
        start = (((2 * i + bit) ^ dp) * n_ctx + (to ^ dev)) * col
        src = g_ref.at[:, pl.ds(pl.multiple_of(start, col), col)]
        return pltpu.make_async_copy(src, dst.at[i, :, pl.ds(to * col, col)], sem.at[where, i * n_ctx + to])

    def each(what, *args):
        for i in range(n_half):
            for to in range(n_ctx):
                getattr(fetch(i, to, *args), what)()

    if core:
        each("start", 1, g_scr, 0)
        each("start", 0, other_ref, 1)
    at = jnp.transpose(a_ref[...])
    for i in range(n_half):
        if core:
            for to in range(n_ctx):
                fetch(i, to, 1, g_scr, 0).wait()
        block = g_scr[i] if core else g_ref[i]
        res = jnp.dot(at, block, preferred_element_type=F32).astype(BF16)
        for to in range(n_ctx):
            part = res[:, to * col : (to + 1) * col]
            outs[i & 1][(i >> 1) * n_ctx + to] = part[:rows]
            outs[2 + ((to >> 1) & 1)][i * (n_ctx // 2) + ((to >> 2) << 1 | (to & 1))] = part[rows:]
    if core:
        each("wait", 0, other_ref, 1)


def home_kernel(n_in, own_ref, cos_ref, sin_ref, *rest):
    ins, (dk_ref, dv_ref) = rest[:n_in], rest[n_in:]
    total = own_ref[...]
    for ref in ins:
        total = total + ref[...].astype(F32)
    dk_ref[...] = rotate(total[:, :HEAD] * SCALE, cos_ref[...], -sin_ref[...]).astype(BF16)
    dv_ref[...] = total[:, HEAD:].astype(BF16)


def final_kernel(bits, owner_ref, one_ref, recv_ref, lse_ref, wgrad_ref, out_ref, all_scr):
    size = one_ref.shape[0]
    wgrad_ref[...] = one_ref[...].astype(F32) + recv_ref[:size].astype(F32)
    dev, n_ctx = place()
    heads, tok = out_ref.shape
    block_len = tok // n_ctx
    count = lse_ref.shape[0]
    all_scr[:count] = lse_ref[...].astype(F32)
    all_scr[count:] = recv_ref[size:].astype(F32)
    each = 2 * count // n_ctx
    chunks = tok // 2 // HEAD
    of_half = heads * chunks
    for c in range(n_ctx):
        away = dev ^ c
        index = jnp.int32(0)
        for k, b in enumerate(bits):
            index = index | (((away >> b) & 1) << k)
        raw = all_scr[pl.ds(pl.multiple_of(index * each, each), each), :]
        mine = jnp.zeros((heads, block_len), F32)
        for s in range(n_ctx):
            half, rest = divmod(s * block_len, tok // 2)
            chunk, lane = divmod(rest, HEAD)
            parts = []
            for h in range(heads):
                row = half * 2 * of_half + h * chunks + chunk
                line = raw[row : row + 1] + raw[row + of_half : row + of_half + 1]
                parts.append(line[:, lane : lane + block_len])
            mine = jnp.where(owner_ref[c * n_ctx + s] == dev, jnp.concatenate(parts, axis=0), mine)
        out_ref[:, c * block_len : (c + 1) * block_len] = mine


SMEM_SPEC = pl.BlockSpec(memory_space=pltpu.SMEM)
VMEM_SPEC = pl.BlockSpec(memory_space=pltpu.VMEM)
ANY_SPEC = pl.BlockSpec(memory_space=pl.ANY)


def params(mib, *semantics):
    return pltpu.CompilerParams(dimension_semantics=semantics or None, vmem_limit_bytes=mib << 20)


def cost(flops, size, exps=0):
    return pl.CostEstimate(flops=int(flops), bytes_accessed=int(size), transcendentals=int(exps))


def after(x, *others):
    return lax.optimization_barrier((x, *others))[0]


def on_device(queries, keys, values, doc_lengths, owner, out_weight, out_grad):
    n_ctx = lax.axis_size("ctx")
    n_dp = lax.axis_size("dp")
    dev = lax.axis_index("ctx").astype(jnp.int32)
    dp = lax.axis_index("dp").astype(jnp.int32)
    tok = queries.shape[1]
    width = queries.shape[2]
    heads = width // HEAD
    seq_len = tok * n_ctx
    d_model = out_grad.shape[2]
    reach = min(WIN, seq_len // 2)
    back = min(-(-reach // tok), n_ctx - 1)
    sds = jax.ShapeDtypeStruct

    half = HEAD // 2
    freq = (10000.0 ** (-2.0 * np.arange(half) / HEAD)).astype(np.float32)
    freq = jnp.asarray(np.concatenate([freq, freq])[None, :])

    def shift(x, pairs):
        return lax.ppermute(x, "ctx", pairs)

    hop = [(i, i + 2) for i in range(n_ctx - 2)]
    hop_back = [(b, a) for a, b in hop]
    up = [(i, i + 1) for i in range(0, n_ctx, 2)]
    down = [(b, a) for a, b in up]
    swap = up + down
    odd = dev % 2 == 1
    paired = is_paired(n_ctx, back)

    kv_home, cos, sin = pl.pallas_call(
        prep_kernel,
        out_shape=(sds((tok, 2 * HEAD), BF16), sds((tok, HEAD), F32), sds((tok, HEAD), F32)),
        in_specs=[SMEM_SPEC] + [VMEM_SPEC] * 3,
        out_specs=(VMEM_SPEC,) * 3,
        compiler_params=params(58),
        cost_estimate=cost(1 << 22, 1 << 20),
        name="prep",
    )(doc_lengths, freq, keys[0], values[0])

    def d_out_of(grad):
        return lax.dot_general(
            grad, out_weight, (((1,), (1,)), ((), ())), preferred_element_type=F32
        ).astype(BF16)

    def rotated_queries(x):
        return pl.pallas_call(
            rotq_kernel,
            out_shape=sds((tok, width), BF16),
            in_specs=[VMEM_SPEC] * 3,
            out_specs=VMEM_SPEC,
            compiler_params=params(4),
            cost_estimate=cost(1 << 22, 2 << 20),
            name="rotq",
        )(x, cos, sin)

    qb = tok // 2
    kb = tok
    tok_spec = pl.BlockSpec((qb, width), lambda i: (i, 0))
    lse_spec = pl.BlockSpec((heads, qb), lambda i: (0, i))
    table_spec = pl.BlockSpec((qb, HEAD), lambda i: (i, 0))
    dq_spec = pl.BlockSpec((1, HEAD, heads * qb), lambda i: (i, 0, 0))
    stat_spec = pl.BlockSpec((1, 16, heads * qb), lambda i: (i, 0, 0))
    pairs = heads * tok * (tok + reach) // 2
    pack_rows = 2 * heads * qb // HEAD
    steps = tok // qb
    state = [(sds((steps, HEAD, heads * qb), F32), dq_spec), (sds((steps, 16, heads * qb), F32), stat_spec)]
    result = [
        (sds((tok, width), BF16), tok_spec),
        (sds((tok, width), BF16), tok_spec),
        (sds((heads, tok), F32), lse_spec),
        (sds((steps, pack_rows, HEAD), BF16), pl.BlockSpec((1, pack_rows, HEAD), lambda i: (i, 0, 0))),
    ]

    def forward(picks, taken, before, finish):
        outs = result if finish else state
        return pl.pallas_call(
            functools.partial(fwd_kernel, picks, back, bool(before), finish),
            grid=(steps,),
            out_shape=[o[0] for o in outs],
            in_specs=[SMEM_SPEC, tok_spec] + [ANY_SPEC] * len(taken) + [s[1] for s in state] * bool(before),
            out_specs=[o[1] for o in outs],
            scratch_shapes=[
                pltpu.VMEM((len(taken), tok, 2 * HEAD), BF16),
                pltpu.SemaphoreType.DMA((len(taken),)),
            ],
            compiler_params=params(FWD_MIB, "arbitrary"),
            cost_estimate=cost(2 * pairs * HEAD, 4 << 20, pairs // 2),
        )(doc_lengths, q_rot, *taken, *before)

    if paired:
        a1 = shift(kv_home, hop)
        e1 = shift(kv_home, up)
        q_rot = rotated_queries(queries[0])
        s1 = shift(a1, swap)
        a2 = shift(a1, hop)
        partial = forward((0, 1, 2), [kv_home, a1, e1], [], False)
        o3 = shift(a2, down)
        d_out = d_out_of(after(out_grad[0], a2))
        blocks = [kv_home, a1, e1, a2, s1, o3]
        attn_out, attn, lse, pack = forward((3, 4, 5), [a2, s1, o3], partial, True)
    else:
        blocks = [kv_home] + [
            shift(kv_home, [(i, i + s) for i in range(n_ctx - s)]) for s in range(1, back + 1)
        ]
        q_rot = rotated_queries(queries[0])
        d_out = d_out_of(out_grad[0])
        attn_out, attn, lse, pack = forward(tuple(range(back + 1)), blocks, [], True)

    col = d_model // (n_dp * n_ctx)
    bits_dp = n_dp.bit_length() - 1
    bits_ctx = n_ctx.bit_length() - 1
    rows = width // 2
    n_half = n_dp // 2
    wide = n_ctx * col

    def shapes_of(sizes):
        return [sds((size, rows, col), BF16) for size in sizes]

    sizes = [n_half // 2 * n_ctx] * 2 + [n_half * n_ctx // 2] * 2

    def partial_wo(core, grads):
        return pl.pallas_call(
            functools.partial(wo_kernel, core),
            out_shape=shapes_of(sizes) + ([sds((n_half, tok, wide), BF16)] if core else []),
            in_specs=[VMEM_SPEC, ANY_SPEC if core else VMEM_SPEC],
            out_specs=[VMEM_SPEC] * (4 + core),
            scratch_shapes=[
                pltpu.VMEM((n_half, tok, wide), BF16),
                pltpu.SemaphoreType.DMA((2, n_half * n_ctx)),
            ],
            compiler_params=params(WO_MIB),
            cost_estimate=cost(tok * width * d_model, 6 << 20),
        )(attn, grads)

    def partial_wo_narrow(core):
        grads = out_grad[0].reshape(tok, n_dp, n_ctx, col)
        grads = jnp.take(grads, (2 * jnp.arange(n_half) + core) ^ dp, axis=1)
        grads = jnp.take(grads, jnp.arange(n_ctx) ^ dev, axis=2)
        res = jnp.einsum("tr,tabc->abrc", attn, grads, preferred_element_type=F32).astype(BF16)
        upper = res[:, :, :rows].reshape(n_half // 2, 2, n_ctx, rows, col)
        lower = res[:, :, rows:].reshape(n_half, n_ctx // 4, 2, 2, rows, col)
        outs = [upper[:, w].reshape(-1, rows, col) for w in range(2)]
        return outs + [lower[:, :, w].reshape(-1, rows, col) for w in range(2)]

    def exchange(x, axis, bit, size):
        return lax.ppermute(x, axis, [(i, i ^ bit) for i in range(size)])

    size_of = {"dp": n_dp, "ctx": n_ctx}
    lead = [("dp", b) for b in range(bits_dp - 1, 0, -1)]
    lead += [("ctx", b) for b in range(bits_ctx - 1, -1, -1)]

    def move(x, axis):
        return exchange(x, axis[0], 1 << axis[1], size_of[axis[0]])

    class Parts:
        def __init__(self, addends, left):
            self.left = list(left)
            self.addends = [x.reshape((2,) * len(self.left) + x.shape[-2:]) for x in addends]

        def pick(self, axis, which):
            at = self.left.index(axis)
            picked = [lax.index_in_dim(x, which, at, keepdims=False) for x in self.addends]
            return functools.reduce(jnp.add, [x.astype(F32) for x in picked]).astype(BF16)

        def step(self, axis, recv):
            at = self.left.index(axis)
            kept = [lax.index_in_dim(x, 0, at, keepdims=False) for x in self.addends]
            return Parts(kept + [recv], [a for a in self.left if a != axis])

    firsts = [("dp", 1), ("ctx", 1)]
    if col % HEAD == 0:
        *wo_send, grads_keep = partial_wo(1, out_grad[0])
        wo_recv = [None] * 4
        for n in (1, 3, 0, 2):
            wo_recv[n] = exchange(wo_send[n], "dp", 1, n_dp)
        wo_keep = partial_wo(0, grads_keep)
    else:
        wo_recv = [exchange(x, "dp", 1, n_dp) for x in partial_wo_narrow(1)]
        wo_keep = partial_wo_narrow(0)
    lefts = [[a for a in lead if a != firsts[c]] for c in range(2)]
    sends = []
    color = []
    for c in range(2):
        kept, sent = [Parts([wo_keep[2 * c + w], wo_recv[2 * c + w]], lefts[c]) for w in range(2)]
        color.append(kept)
        total = functools.reduce(jnp.add, [x.astype(F32) for x in sent.addends]).astype(BF16)
        sends.append(total)

    lines = pack.reshape(-1, col)

    def with_lse(x, lse_of):
        return jnp.concatenate([x.reshape(-1, col), lse_of], axis=0)

    recv = move(sends[0], firsts[0])
    color[0] = Parts(color[0].addends + [recv], lefts[0])
    size = sends[1].size // col
    recv = move(with_lse(sends[1], lines), firsts[1])
    color[1] = Parts(color[1].addends + [recv[:size].reshape(sends[1].shape)], lefts[1])
    lines = jnp.concatenate([lines, recv[size:]], axis=0)

    def backward_far(lo, hi, lse_in, third, dq_in):
        count = hi - lo
        new = [] if dq_in else [(sds((heads, tok), F32), lse_spec)]
        return pl.pallas_call(
            functools.partial(far_kernel, len(blocks) - 1, back, lo, len(dq_in), kb),
            grid=(tok // qb,),
            out_shape=[sds((tok // qb, HEAD, heads * qb), F32), sds((count, tok, 2 * HEAD), BF16)]
            + [n[0] for n in new],
            in_specs=[SMEM_SPEC, tok_spec, tok_spec, lse_spec if dq_in else tok_spec, lse_spec]
            + [ANY_SPEC] * (len(blocks) - 1)
            + [dq_spec] * len(dq_in),
            out_specs=[dq_spec, pl.BlockSpec((count, tok, 2 * HEAD), lambda i: (0, 0, 0))]
            + [n[1] for n in new],
            scratch_shapes=[
                pltpu.VMEM((count * tok, 2 * HEAD), BF16),
                pltpu.VMEM((count * tok, HEAD), F32),
                pltpu.VMEM((count * tok, HEAD), F32),
                pltpu.SemaphoreType.DMA((len(blocks) - 1,)),
            ],
            compiler_params=params(FAR_MIB, "arbitrary"),
            cost_estimate=cost(8 * pairs * HEAD, 8 << 20, pairs),
        )(doc_lengths, q_rot, d_out, third, lse_in, *blocks[1:], *dq_in)

    def plus(*xs):
        return functools.reduce(jnp.add, [x.astype(F32) for x in xs]).astype(BF16)

    lse_b = after(lse, *sends)
    if paired:
        dq_far, (d4, d3), delta = backward_far(0, 2, lse_b, attn, [])
        r3 = shift(d3, swap)
        dq_far, (d2, d1) = backward_far(2, 4, lse_b, delta, [dq_far])
        none = jnp.zeros_like(r3)
        sum4 = plus(d4, jnp.where(odd, r3, none))
        b2 = shift(sum4, hop_back)
        r1 = shift(d1, swap)
    else:
        dq_far, far, delta = backward_far(0, back, lse_b, attn, [])

    seconds = [firsts[1], firsts[0]]
    extra = [a for a in lead if a[0] == "dp" and a not in firsts]
    sends = []
    for c in range(2):
        color[c].addends[-1] = after(color[c].addends[-1], dq_far)
        for axis in [seconds[c]] + extra:
            sends.append(color[c].pick(axis, 1))
            color[c] = color[c].step(axis, move(sends[-1], axis))

    dq_near = after(dq_far, *sends)
    near_kb = max(kb // 2, 8)
    q_grad, own = pl.pallas_call(
        functools.partial(near_kernel, near_kb),
        grid=(tok // qb,),
        out_shape=(sds((tok, width), BF16), sds((tok, 2 * HEAD), F32)),
        in_specs=[SMEM_SPEC, tok_spec, tok_spec, lse_spec, lse_spec, dq_spec, VMEM_SPEC, table_spec, table_spec],
        out_specs=(tok_spec, pl.BlockSpec((tok, 2 * HEAD), lambda i: (0, 0))),
        scratch_shapes=[pltpu.VMEM((tok, HEAD), F32), pltpu.VMEM((tok, HEAD), F32)],
        compiler_params=params(NEAR_MIB, "arbitrary"),
        cost_estimate=cost(8 * heads * tok * tok * HEAD, 4 << 20, heads * tok * tok),
        name="near",
    )(doc_lengths, q_rot, d_out, delta, lse, dq_near, kv_home, cos, sin)

    ctx_axes = [("ctx", 0)] + [("ctx", b) for b in range(2, bits_ctx)]
    lse_bits = [1, 0] + list(range(2, bits_ctx))
    both = None
    for axis in ctx_axes:
        if both is None:
            pieces = [jnp.concatenate([color[c].pick(axis, w) for c in range(2)], axis=-2) for w in range(2)]
            left = [a for a in color[0].left if a != axis]
            send = after(pieces[1], own)
            kept = [pieces[0]]
        else:
            send = both.pick(axis, 1)
            left = [a for a in both.left if a != axis]
            at = both.left.index(axis)
            kept = [lax.index_in_dim(x, 0, at, keepdims=False) for x in both.addends]
        size = send.size // col
        recv = move(with_lse(send, lines), axis)
        if axis != ctx_axes[-1]:
            both = Parts(kept + [recv[:size].reshape(send.shape)], left)
            lines = jnp.concatenate([lines, recv[size:]], axis=0)
    last = functools.reduce(jnp.add, [x.astype(F32) for x in kept]).astype(BF16)

    if paired:
        sum2 = plus(d2, b2, jnp.where(odd, r1, r3))
        arrived = [shift(after(sum2, own), hop_back), jnp.where(odd, none, r1)]
    else:
        arrived = [
            shift(far[back - s], [(i + s, i) for i in range(n_ctx - s)]) for s in range(1, back + 1)
        ]
    k_grad, v_grad = pl.pallas_call(
        functools.partial(home_kernel, len(arrived)),
        out_shape=(sds((tok, HEAD), BF16), sds((tok, HEAD), BF16)),
        in_specs=[VMEM_SPEC] * (3 + len(arrived)),
        out_specs=(VMEM_SPEC, VMEM_SPEC),
        compiler_params=params(4),
        cost_estimate=cost(1 << 20, 2 << 20),
        name="home",
    )(own, cos, sin, *arrived)

    if col != HEAD:
        tail_rows = recv[width:].reshape(-1, HEAD)
        recv = jnp.concatenate([jnp.pad(recv[:width], ((0, 0), (0, HEAD - col))), tail_rows], axis=0)
        last = jnp.pad(last, ((0, 0), (0, HEAD - col)))
        lines = lines.reshape(-1, HEAD)
    wgrad, owner_lse = pl.pallas_call(
        functools.partial(final_kernel, lse_bits),
        out_shape=(sds((width, HEAD), F32), sds((heads, tok), F32)),
        in_specs=[SMEM_SPEC] + [VMEM_SPEC] * 3,
        out_specs=(VMEM_SPEC,) * 2,
        scratch_shapes=[pltpu.VMEM((2 * lines.size // HEAD, HEAD), F32)],
        compiler_params=params(8),
        cost_estimate=cost(1 << 18, 1 << 20),
        name="final",
    )(owner[0], last, recv, lines)
    wgrad = wgrad[:, :col]
    owner_lse = jnp.transpose(owner_lse)

    return (attn_out[None], q_grad[None], k_grad[None], v_grad[None], wgrad, owner_lse[None, None])


def solution(mesh):
    in_specs = (
        P("dp", "ctx", None),
        P("dp", "ctx", None),
        P("dp", "ctx", None),
        P("dp", None),
        P("dp", None),
        P(),
        P("dp", "ctx", None),
    )
    out_specs = (
        P("dp", "ctx", None),
        P("dp", "ctx", None),
        P("dp", "ctx", None),
        P("dp", "ctx", None),
        P(None, ("dp", "ctx")),
        P("dp", "ctx", None, None),
    )

    return jax.shard_map(on_device, mesh=mesh, in_specs=in_specs, out_specs=out_specs, check_vma=False)
```

```python
import functools
import math

import numpy as np

import jax
import jax.numpy as jnp
from jax import lax
from jax.experimental import pallas as pl
from jax.experimental.pallas import tpu as pltpu
from jax.sharding import PartitionSpec as P


HEAD = 128
WIN = 4096
NEG = -1e30
LOG2E = math.log2(math.e)
LN2 = math.log(2.0)
SCALE = 1.0 / math.sqrt(HEAD)
FWD_MIB, WO_MIB, FAR_MIB, NEAR_MIB = 16, 14, 20, 14
F32 = jnp.float32
BF16 = jnp.bfloat16


def doc_starts(lens_ref, pos):
    begin = jnp.int32(0)
    found = jnp.zeros_like(pos)
    for d in range(lens_ref.shape[1]):
        found = jnp.where(pos >= begin, begin, found)
        begin = begin + lens_ref[0, d]
    return found


def sincos(angle):
    turns = jnp.floor(angle * (2.0 / math.pi) + 0.5)
    rest = angle - turns * 1.5703125
    rest = rest - turns * 4.83751296997070312e-4
    rest = rest - turns * 7.54978995489188216e-8
    square = rest * rest
    sine = rest + rest * square * (
        -1.6666654611e-1 + square * (8.3321608736e-3 + square * -1.9515295891e-4)
    )
    cosine = (
        1.0
        - 0.5 * square
        + square
        * square
        * (4.166664568298827e-2 + square * (-1.388731625493765e-3 + square * 2.443315711809948e-5))
    )
    quarter = turns.astype(jnp.int32) & 3
    odd = (quarter & 1) == 1
    out_sin = jnp.where(odd, cosine, sine)
    out_cos = jnp.where(odd, sine, cosine)
    out_sin = jnp.where(quarter >= 2, -out_sin, out_sin)
    out_cos = jnp.where((quarter == 1) | (quarter == 2), -out_cos, out_cos)
    return out_sin, out_cos


def place():
    return lax.axis_index("ctx").astype(jnp.int32), lax.axis_size("ctx")


def rotate(x, cosine, sine):
    return x * cosine + pltpu.roll(x, HEAD // 2, 1) * sine


def prep_kernel(lens_ref, freq_ref, k_ref, v_ref, kv_ref, cos_ref, sin_ref):
    rows = k_ref.shape[0]
    dev, _ = place()
    pos = dev * rows + lax.broadcasted_iota(jnp.int32, (rows, HEAD), 0)
    rel = pos - doc_starts(lens_ref, pos)
    sine, cosine = sincos(rel.astype(F32) * freq_ref[...])
    lane = lax.broadcasted_iota(jnp.int32, (rows, HEAD), 1)
    sine = jnp.where(lane < HEAD // 2, -sine, sine)
    cos_ref[...] = cosine
    sin_ref[...] = sine
    kv_ref[:, :HEAD] = rotate(k_ref[...].astype(F32), cosine, sine).astype(BF16)
    kv_ref[:, HEAD:] = v_ref[...]


def rotq_kernel(q_ref, cos_ref, sin_ref, out_ref):
    for h in range(q_ref.shape[1] // HEAD):
        q = q_ref[:, h * HEAD : (h + 1) * HEAD].astype(F32)
        out_ref[:, h * HEAD : (h + 1) * HEAD] = rotate(q, cos_ref[...], sin_ref[...]).astype(BF16)


def is_paired(n_ctx, back):
    return n_ctx == 8 and back == 4


def slot_list(dev, n_ctx, back):
    if is_paired(n_ctx, back):
        odd = dev % 2 == 1
        skip = jnp.int32(-1)
        return [4, 2, jnp.where(odd, 3, skip), 0, jnp.where(odd, 1, 3), jnp.where(odd, skip, 1)]
    return [back - s for s in range(back + 1)]


def load_slots(slots, refs, scratch, sem, rows, lo=0):
    hi = lo + scratch.shape[0] // rows
    for start in (True, False):
        for i, (slot, ref) in enumerate(zip(slots, refs)):
            if isinstance(slot, int) and not lo <= slot < hi:
                continue

            def move(slot=slot, ref=ref, i=i):
                at = (slot - lo) * rows
                if not isinstance(at, int):
                    at = pl.multiple_of(at, rows)
                copy = pltpu.make_async_copy(ref, scratch.at[pl.ds(at, rows)], sem.at[i])
                if start:
                    copy.start()
                else:
                    copy.wait()

            if isinstance(slot, int):
                move()
            else:
                pl.when((slot >= lo) & (slot < hi))(move)


def tile_ranges(lens_ref, first, qb, kb, base, n_tiles):
    last = first + qb - 1
    low_first = jnp.maximum(doc_starts(lens_ref, first), first - WIN + 1)
    low_last = jnp.maximum(doc_starts(lens_ref, last), last - WIN + 1)
    hi = jnp.minimum((last - base) // kb + 1, n_tiles)
    lo = jnp.minimum(jnp.maximum(low_first - base, 0) // kb, hi)
    full_lo = jnp.clip((jnp.maximum(low_last - base, 0) + kb - 1) // kb, lo, hi)
    full_hi = jnp.clip((first - base + 1) // kb, full_lo, hi)
    return lo, full_lo, full_hi, hi


def over_tiles(ranges, visit, carry):
    lo, full_lo, full_hi, hi = ranges
    carry = lax.fori_loop(full_lo, full_hi, functools.partial(visit, False), carry)

    def edge(i, c):
        return visit(True, jnp.where(lo + i < full_lo, lo + i, full_hi + i - (full_lo - lo)), c)

    return lax.fori_loop(0, (full_lo - lo) + (hi - full_hi), edge, carry)


def fold(x, op):
    return op(x.reshape(x.shape[0] // 8, 8, x.shape[1]), axis=0)


def stack_heads(ref):
    heads = ref.shape[1] // HEAD
    return jnp.concatenate([ref[:, h * HEAD : (h + 1) * HEAD] for h in range(heads)], axis=0)


def query_bounds(lens_ref, first, qb, heads):
    pos = first + lax.broadcasted_iota(jnp.int32, (1, qb), 1)
    low = jnp.maximum(doc_starts(lens_ref, pos), pos - WIN + 1)
    return jnp.concatenate([low] * heads, axis=1), jnp.concatenate([pos] * heads, axis=1)


def masked_scores(s, base, at, low, high):
    key = base + at + lax.broadcasted_iota(jnp.int32, (s.shape[0], 1), 0)
    return jnp.where((key >= low) & (key <= high), s, NEG)


NT = (((1,), (1,)), ((), ()))
NN = (((1,), (0,)), ((), ()))
TN = (((0,), (0,)), ((), ()))


def dot(a, b, dims):
    return lax.dot_general(a, b, dims, preferred_element_type=F32)


def fwd_kernel(picks, back, resume, finish, lens_ref, q_ref, *rest):
    kv_refs, rest = rest[: len(picks)], rest[len(picks) :]
    if resume:
        acc_in_ref, stat_in_ref, *rest = rest
    *outs, kv_scr, sem = rest
    step = pl.program_id(0)
    qb, width = q_ref.shape
    heads = width // HEAD
    rows = heads * qb
    kb = kv_refs[0].shape[0]
    dev, n_ctx = place()
    slots = [slot_list(dev, n_ctx, back)[p] for p in picks]

    @pl.when(step == 0)
    def _():
        copies = [
            pltpu.make_async_copy(ref, kv_scr.at[i], sem.at[i]) for i, ref in enumerate(kv_refs)
        ]
        for copy in copies:
            copy.start()
        for copy in copies:
            copy.wait()

    base = (dev - back) * kb
    first = dev * kb + step * qb
    q = stack_heads(q_ref)
    low, high = query_bounds(lens_ref, first, qb, heads)
    factor = SCALE * LOG2E
    lo, full_lo, full_hi, hi = tile_ranges(lens_ref, first, qb, kb, base, back + 1)

    def visit(masked, i, slot, carry):
        top, total, acc = carry
        s = dot(kv_scr[i, :, :HEAD], q, NT)
        if masked:
            s = masked_scores(s, base, slot * kb, low, high)
        new = jnp.maximum(top, jnp.max(fold(s, jnp.max), axis=0, keepdims=True) * factor)
        alpha = jnp.exp2(top - new)
        p = jnp.exp2(s * factor - new)
        total = total * alpha + fold(p, jnp.sum)
        acc = acc * alpha + dot(kv_scr[i, :, HEAD:], p.astype(BF16), TN)
        return new, total, acc

    def block(i, carry):
        slot = jnp.int32(slots[0])
        for n in range(1, len(slots)):
            slot = jnp.where(i == n, slots[n], slot)
        seen = (slot >= lo) & (slot < hi)
        full = seen & (slot >= full_lo) & (slot < full_hi)
        for masked, go in ((False, full), (True, seen & ~full)):
            carry = lax.fori_loop(
                0, go.astype(jnp.int32), lambda _, c, masked=masked: visit(masked, i, slot, c), carry
            )
        return carry

    if resume:
        carry = (stat_in_ref[0, 0:1], stat_in_ref[0, 8:16], acc_in_ref[0])
    else:
        carry = (jnp.full((1, rows), NEG, F32), jnp.zeros((8, rows), F32), jnp.zeros((HEAD, rows), F32))
    top, total, acc = lax.fori_loop(0, len(picks), block, carry)
    if not finish:
        acc_ref, stat_ref = outs
        acc_ref[0] = acc
        stat_ref[0, 0:8] = jnp.broadcast_to(top, (8, rows))
        stat_ref[0, 8:16] = total
        return
    o_ref, keep_ref, lse_ref, pack_ref = outs
    total = jnp.sum(total, axis=0, keepdims=True)
    lse = (top + jnp.log2(total)) * LN2
    out = acc / total
    for h in range(heads):
        lse_ref[h : h + 1, :] = lse[:, h * qb : (h + 1) * qb]
        part = jnp.transpose(out[:, h * qb : (h + 1) * qb]).astype(BF16)
        o_ref[:, h * HEAD : (h + 1) * HEAD] = part
        keep_ref[:, h * HEAD : (h + 1) * HEAD] = part
    lines = jnp.concatenate(
        [lse[:, c * HEAD : (c + 1) * HEAD] for c in range(rows // HEAD)], axis=0
    )
    pack_ref[0] = lines.astype(BF16)


def delta_of(dy_ref, o_ref):
    prod = stack_heads(dy_ref).astype(F32) * stack_heads(o_ref).astype(F32)
    qb = dy_ref.shape[0]
    return [
        jnp.sum(jnp.transpose(prod[i : i + qb]), axis=0, keepdims=True)
        for i in range(0, prod.shape[0], qb)
    ]


def bwd_core(lens_ref, q_ref, dy_ref, delta_ref, lse_ref, kv, base, kb, dk_scr, dv_scr, dq):
    qb, width = q_ref.shape
    heads = width // HEAD
    tok = qb * pl.num_programs(0)
    dev, _ = place()
    first = dev * tok + pl.program_id(0) * qb
    q, dy = stack_heads(q_ref), stack_heads(dy_ref)
    lse = jnp.concatenate([lse_ref[h : h + 1, :] for h in range(heads)], axis=1) * LOG2E
    delta = jnp.concatenate([delta_ref[h : h + 1, :] for h in range(heads)], axis=1)
    low, high = query_bounds(lens_ref, first, qb, heads)
    factor = SCALE * LOG2E

    def visit(masked, j, dq):
        at = pl.multiple_of(j * kb, kb)
        k, v = kv[pl.ds(at, kb), :HEAD], kv[pl.ds(at, kb), HEAD:]
        s = dot(k, q, NT)
        if masked:
            s = masked_scores(s, base, at, low, high)
        p = jnp.exp2(s * factor - lse)
        ds = (p * (dot(v, dy, NT) - delta)).astype(BF16)
        dv_scr[pl.ds(at, kb), :] += dot(p.astype(BF16), dy, NN)
        dk_scr[pl.ds(at, kb), :] += dot(ds, q, NN)
        return dq + dot(k, ds, TN)

    return over_tiles(tile_ranges(lens_ref, first, qb, kb, base, kv.shape[0] // kb), visit, dq)


def far_kernel(n_refs, back, lo, has_dq, kb, lens_ref, q_ref, dy_ref, o_ref, lse_ref, *rest):
    kv_refs = rest[:n_refs]
    dqin_ref = rest[n_refs] if has_dq else None
    dq_ref, far_ref, *rest = rest[n_refs + has_dq :]
    if has_dq:
        delta_ref = o_ref
    else:
        delta_ref, *rest = rest
        for h, line in enumerate(delta_of(dy_ref, o_ref)):
            delta_ref[h : h + 1, :] = line
    kv_scr, dk_scr, dv_scr, sem = rest
    tok = kv_refs[0].shape[0]
    dev, n_ctx = place()
    step = pl.program_id(0)

    @pl.when(step == 0)
    def _():
        load_slots(slot_list(dev, n_ctx, back)[1:], kv_refs, kv_scr, sem, tok, lo)
        dk_scr[...] = jnp.zeros_like(dk_scr)
        dv_scr[...] = jnp.zeros_like(dv_scr)

    base = (dev - back + lo) * tok
    dq = dqin_ref[0] if has_dq else jnp.zeros(dq_ref.shape[1:], F32)
    dq_ref[0] = bwd_core(
        lens_ref, q_ref, dy_ref, delta_ref, lse_ref, kv_scr, base, kb, dk_scr, dv_scr, dq
    )

    @pl.when(step == pl.num_programs(0) - 1)
    def _():
        for r in range(far_ref.shape[0]):
            far_ref[r, :, :HEAD] = dk_scr[r * tok : (r + 1) * tok, :].astype(BF16)
            far_ref[r, :, HEAD:] = dv_scr[r * tok : (r + 1) * tok, :].astype(BF16)


def near_kernel(kb, lens_ref, q_ref, dy_ref, delta_ref, lse_ref, dqin_ref, kv_ref, cos_ref, sin_ref,
                dq_ref, own_ref, dk_scr, dv_scr):
    tok = kv_ref.shape[0]
    dev, _ = place()
    step = pl.program_id(0)
    qb = q_ref.shape[0]

    @pl.when(step == 0)
    def _():
        dk_scr[...] = jnp.zeros_like(dk_scr)
        dv_scr[...] = jnp.zeros_like(dv_scr)

    dq = bwd_core(
        lens_ref, q_ref, dy_ref, delta_ref, lse_ref, kv_ref, dev * tok, kb, dk_scr, dv_scr, dqin_ref[0]
    )
    for h in range(q_ref.shape[1] // HEAD):
        part = jnp.transpose(dq[:, h * qb : (h + 1) * qb]) * SCALE
        dq_ref[:, h * HEAD : (h + 1) * HEAD] = rotate(part, cos_ref[...], -sin_ref[...]).astype(BF16)

    @pl.when(step == pl.num_programs(0) - 1)
    def _():
        own_ref[:, :HEAD] = dk_scr[...]
        own_ref[:, HEAD:] = dv_scr[...]


def wo_kernel(core, a_ref, g_ref, *rest):
    g_scr, sem = rest[-2:]
    outs, other_ref = rest[:4], (rest[4] if core else None)
    dev, n_ctx = place()
    dp = lax.axis_index("dp").astype(jnp.int32)
    _, wide = g_scr.shape[1:]
    n_half = g_scr.shape[0]
    col = wide // n_ctx
    rows = outs[0].shape[1]

    def fetch(i, to, bit, dst, where):
        start = (((2 * i + bit) ^ dp) * n_ctx + (to ^ dev)) * col
        src = g_ref.at[:, pl.ds(pl.multiple_of(start, col), col)]
        return pltpu.make_async_copy(src, dst.at[i, :, pl.ds(to * col, col)], sem.at[where, i * n_ctx + to])

    def each(what, *args):
        for i in range(n_half):
            for to in range(n_ctx):
                getattr(fetch(i, to, *args), what)()

    if core:
        each("start", 1, g_scr, 0)
        each("start", 0, other_ref, 1)
    at = jnp.transpose(a_ref[...])
    for i in range(n_half):
        if core:
            for to in range(n_ctx):
                fetch(i, to, 1, g_scr, 0).wait()
        block = g_scr[i] if core else g_ref[i]
        res = jnp.dot(at, block, preferred_element_type=F32).astype(BF16)
        for to in range(n_ctx):
            part = res[:, to * col : (to + 1) * col]
            outs[i & 1][(i >> 1) * n_ctx + to] = part[:rows]
            outs[2 + ((to >> 1) & 1)][i * (n_ctx // 2) + ((to >> 2) << 1 | (to & 1))] = part[rows:]
    if core:
        each("wait", 0, other_ref, 1)


def home_kernel(n_in, own_ref, cos_ref, sin_ref, *rest):
    ins, (dk_ref, dv_ref) = rest[:n_in], rest[n_in:]
    total = own_ref[...]
    for ref in ins:
        total = total + ref[...].astype(F32)
    dk_ref[...] = rotate(total[:, :HEAD] * SCALE, cos_ref[...], -sin_ref[...]).astype(BF16)
    dv_ref[...] = total[:, HEAD:].astype(BF16)


def final_kernel(bits, owner_ref, one_ref, recv_ref, lse_ref, wgrad_ref, out_ref, all_scr):
    size = one_ref.shape[0]
    wgrad_ref[...] = one_ref[...].astype(F32) + recv_ref[:size].astype(F32)
    dev, n_ctx = place()
    heads, tok = out_ref.shape
    block_len = tok // n_ctx
    count = lse_ref.shape[0]
    all_scr[:count] = lse_ref[...].astype(F32)
    all_scr[count:] = recv_ref[size:].astype(F32)
    each = 2 * count // n_ctx
    chunks = tok // 2 // HEAD
    of_half = heads * chunks
    for c in range(n_ctx):
        away = dev ^ c
        index = jnp.int32(0)
        for k, b in enumerate(bits):
            index = index | (((away >> b) & 1) << k)
        raw = all_scr[pl.ds(pl.multiple_of(index * each, each), each), :]
        mine = jnp.zeros((heads, block_len), F32)
        for s in range(n_ctx):
            half, rest = divmod(s * block_len, tok // 2)
            chunk, lane = divmod(rest, HEAD)
            parts = []
            for h in range(heads):
                row = half * of_half + h * chunks + chunk
                line = raw[row : row + 1]
                parts.append(line[:, lane : lane + block_len])
            mine = jnp.where(owner_ref[c * n_ctx + s] == dev, jnp.concatenate(parts, axis=0), mine)
        out_ref[:, c * block_len : (c + 1) * block_len] = mine


SMEM_SPEC = pl.BlockSpec(memory_space=pltpu.SMEM)
VMEM_SPEC = pl.BlockSpec(memory_space=pltpu.VMEM)
ANY_SPEC = pl.BlockSpec(memory_space=pl.ANY)


def params(mib, *semantics):
    return pltpu.CompilerParams(dimension_semantics=semantics or None, vmem_limit_bytes=mib << 20)


def cost(flops, size, exps=0):
    return pl.CostEstimate(flops=int(flops), bytes_accessed=int(size), transcendentals=int(exps))


def after(x, *others):
    return lax.optimization_barrier((x, *others))[0]


def on_device(queries, keys, values, doc_lengths, owner, out_weight, out_grad):
    n_ctx = lax.axis_size("ctx")
    n_dp = lax.axis_size("dp")
    dev = lax.axis_index("ctx").astype(jnp.int32)
    dp = lax.axis_index("dp").astype(jnp.int32)
    tok = queries.shape[1]
    width = queries.shape[2]
    heads = width // HEAD
    seq_len = tok * n_ctx
    d_model = out_grad.shape[2]
    reach = min(WIN, seq_len // 2)
    back = min(-(-reach // tok), n_ctx - 1)
    sds = jax.ShapeDtypeStruct

    half = HEAD // 2
    freq = (10000.0 ** (-2.0 * np.arange(half) / HEAD)).astype(np.float32)
    freq = jnp.asarray(np.concatenate([freq, freq])[None, :])

    def shift(x, pairs):
        return lax.ppermute(x, "ctx", pairs)

    hop = [(i, i + 2) for i in range(n_ctx - 2)]
    hop_back = [(b, a) for a, b in hop]
    up = [(i, i + 1) for i in range(0, n_ctx, 2)]
    down = [(b, a) for a, b in up]
    swap = up + down
    odd = dev % 2 == 1
    paired = is_paired(n_ctx, back)

    kv_home, cos, sin = pl.pallas_call(
        prep_kernel,
        out_shape=(sds((tok, 2 * HEAD), BF16), sds((tok, HEAD), F32), sds((tok, HEAD), F32)),
        in_specs=[SMEM_SPEC] + [VMEM_SPEC] * 3,
        out_specs=(VMEM_SPEC,) * 3,
        compiler_params=params(58),
        cost_estimate=cost(1 << 22, 1 << 20),
        name="prep",
    )(doc_lengths, freq, keys[0], values[0])

    def d_out_of(grad):
        return lax.dot_general(
            grad, out_weight, (((1,), (1,)), ((), ())), preferred_element_type=F32
        ).astype(BF16)

    def rotated_queries(x):
        return pl.pallas_call(
            rotq_kernel,
            out_shape=sds((tok, width), BF16),
            in_specs=[VMEM_SPEC] * 3,
            out_specs=VMEM_SPEC,
            compiler_params=params(4),
            cost_estimate=cost(1 << 22, 2 << 20),
            name="rotq",
        )(x, cos, sin)

    qb = tok // 2
    kb = tok
    tok_spec = pl.BlockSpec((qb, width), lambda i: (i, 0))
    lse_spec = pl.BlockSpec((heads, qb), lambda i: (0, i))
    table_spec = pl.BlockSpec((qb, HEAD), lambda i: (i, 0))
    dq_spec = pl.BlockSpec((1, HEAD, heads * qb), lambda i: (i, 0, 0))
    stat_spec = pl.BlockSpec((1, 16, heads * qb), lambda i: (i, 0, 0))
    pairs = heads * tok * (tok + reach) // 2
    pack_rows = heads * qb // HEAD
    steps = tok // qb
    state = [(sds((steps, HEAD, heads * qb), F32), dq_spec), (sds((steps, 16, heads * qb), F32), stat_spec)]
    result = [
        (sds((tok, width), BF16), tok_spec),
        (sds((tok, width), BF16), tok_spec),
        (sds((heads, tok), F32), lse_spec),
        (sds((steps, pack_rows, HEAD), BF16), pl.BlockSpec((1, pack_rows, HEAD), lambda i: (i, 0, 0))),
    ]

    def forward(picks, taken, before, finish):
        outs = result if finish else state
        return pl.pallas_call(
            functools.partial(fwd_kernel, picks, back, bool(before), finish),
            grid=(steps,),
            out_shape=[o[0] for o in outs],
            in_specs=[SMEM_SPEC, tok_spec] + [ANY_SPEC] * len(taken) + [s[1] for s in state] * bool(before),
            out_specs=[o[1] for o in outs],
            scratch_shapes=[
                pltpu.VMEM((len(taken), tok, 2 * HEAD), BF16),
                pltpu.SemaphoreType.DMA((len(taken),)),
            ],
            compiler_params=params(FWD_MIB, "arbitrary"),
            cost_estimate=cost(2 * pairs * HEAD, 4 << 20, pairs // 2),
        )(doc_lengths, q_rot, *taken, *before)

    if paired:
        a1 = shift(kv_home, hop)
        e1 = shift(kv_home, up)
        q_rot = rotated_queries(queries[0])
        s1 = shift(a1, swap)
        a2 = shift(a1, hop)
        partial = forward((0, 1, 2), [kv_home, a1, e1], [], False)
        o3 = shift(a2, down)
        d_out = d_out_of(after(out_grad[0], a2))
        blocks = [kv_home, a1, e1, a2, s1, o3]
        attn_out, attn, lse, pack = forward((3, 4, 5), [a2, s1, o3], partial, True)
    else:
        blocks = [kv_home] + [
            shift(kv_home, [(i, i + s) for i in range(n_ctx - s)]) for s in range(1, back + 1)
        ]
        q_rot = rotated_queries(queries[0])
        d_out = d_out_of(out_grad[0])
        attn_out, attn, lse, pack = forward(tuple(range(back + 1)), blocks, [], True)

    col = d_model // (n_dp * n_ctx)
    bits_dp = n_dp.bit_length() - 1
    bits_ctx = n_ctx.bit_length() - 1
    rows = width // 2
    n_half = n_dp // 2
    wide = n_ctx * col

    def shapes_of(sizes):
        return [sds((size, rows, col), BF16) for size in sizes]

    sizes = [n_half // 2 * n_ctx] * 2 + [n_half * n_ctx // 2] * 2

    def partial_wo(core, grads):
        return pl.pallas_call(
            functools.partial(wo_kernel, core),
            out_shape=shapes_of(sizes) + ([sds((n_half, tok, wide), BF16)] if core else []),
            in_specs=[VMEM_SPEC, ANY_SPEC if core else VMEM_SPEC],
            out_specs=[VMEM_SPEC] * (4 + core),
            scratch_shapes=[
                pltpu.VMEM((n_half, tok, wide), BF16),
                pltpu.SemaphoreType.DMA((2, n_half * n_ctx)),
            ],
            compiler_params=params(WO_MIB),
            cost_estimate=cost(tok * width * d_model, 6 << 20),
        )(attn, grads)

    def partial_wo_narrow(core):
        grads = out_grad[0].reshape(tok, n_dp, n_ctx, col)
        grads = jnp.take(grads, (2 * jnp.arange(n_half) + core) ^ dp, axis=1)
        grads = jnp.take(grads, jnp.arange(n_ctx) ^ dev, axis=2)
        res = jnp.einsum("tr,tabc->abrc", attn, grads, preferred_element_type=F32).astype(BF16)
        upper = res[:, :, :rows].reshape(n_half // 2, 2, n_ctx, rows, col)
        lower = res[:, :, rows:].reshape(n_half, n_ctx // 4, 2, 2, rows, col)
        outs = [upper[:, w].reshape(-1, rows, col) for w in range(2)]
        return outs + [lower[:, :, w].reshape(-1, rows, col) for w in range(2)]

    def exchange(x, axis, bit, size):
        return lax.ppermute(x, axis, [(i, i ^ bit) for i in range(size)])

    size_of = {"dp": n_dp, "ctx": n_ctx}
    lead = [("dp", b) for b in range(bits_dp - 1, 0, -1)]
    lead += [("ctx", b) for b in range(bits_ctx - 1, -1, -1)]

    def move(x, axis):
        return exchange(x, axis[0], 1 << axis[1], size_of[axis[0]])

    class Parts:
        def __init__(self, addends, left):
            self.left = list(left)
            self.addends = [x.reshape((2,) * len(self.left) + x.shape[-2:]) for x in addends]

        def pick(self, axis, which):
            at = self.left.index(axis)
            picked = [lax.index_in_dim(x, which, at, keepdims=False) for x in self.addends]
            return functools.reduce(jnp.add, [x.astype(F32) for x in picked]).astype(BF16)

        def step(self, axis, recv):
            at = self.left.index(axis)
            kept = [lax.index_in_dim(x, 0, at, keepdims=False) for x in self.addends]
            return Parts(kept + [recv], [a for a in self.left if a != axis])

    firsts = [("dp", 1), ("ctx", 1)]
    if col % HEAD == 0:
        *wo_send, grads_keep = partial_wo(1, out_grad[0])
        wo_recv = [None] * 4
        for n in (1, 3, 0, 2):
            wo_recv[n] = exchange(wo_send[n], "dp", 1, n_dp)
        wo_keep = partial_wo(0, grads_keep)
    else:
        wo_recv = [exchange(x, "dp", 1, n_dp) for x in partial_wo_narrow(1)]
        wo_keep = partial_wo_narrow(0)
    lefts = [[a for a in lead if a != firsts[c]] for c in range(2)]
    sends = []
    color = []
    for c in range(2):
        kept, sent = [Parts([wo_keep[2 * c + w], wo_recv[2 * c + w]], lefts[c]) for w in range(2)]
        color.append(kept)
        total = functools.reduce(jnp.add, [x.astype(F32) for x in sent.addends]).astype(BF16)
        sends.append(total)

    lines = pack.reshape(-1, col)

    def with_lse(x, lse_of):
        return jnp.concatenate([x.reshape(-1, col), lse_of], axis=0)

    recv = move(sends[0], firsts[0])
    color[0] = Parts(color[0].addends + [recv], lefts[0])
    size = sends[1].size // col
    recv = move(with_lse(sends[1], lines), firsts[1])
    color[1] = Parts(color[1].addends + [recv[:size].reshape(sends[1].shape)], lefts[1])
    lines = jnp.concatenate([lines, recv[size:]], axis=0)

    def backward_far(lo, hi, lse_in, third, dq_in):
        count = hi - lo
        new = [] if dq_in else [(sds((heads, tok), F32), lse_spec)]
        return pl.pallas_call(
            functools.partial(far_kernel, len(blocks) - 1, back, lo, len(dq_in), kb),
            grid=(tok // qb,),
            out_shape=[sds((tok // qb, HEAD, heads * qb), F32), sds((count, tok, 2 * HEAD), BF16)]
            + [n[0] for n in new],
            in_specs=[SMEM_SPEC, tok_spec, tok_spec, lse_spec if dq_in else tok_spec, lse_spec]
            + [ANY_SPEC] * (len(blocks) - 1)
            + [dq_spec] * len(dq_in),
            out_specs=[dq_spec, pl.BlockSpec((count, tok, 2 * HEAD), lambda i: (0, 0, 0))]
            + [n[1] for n in new],
            scratch_shapes=[
                pltpu.VMEM((count * tok, 2 * HEAD), BF16),
                pltpu.VMEM((count * tok, HEAD), F32),
                pltpu.VMEM((count * tok, HEAD), F32),
                pltpu.SemaphoreType.DMA((len(blocks) - 1,)),
            ],
            compiler_params=params(FAR_MIB, "arbitrary"),
            cost_estimate=cost(8 * pairs * HEAD, 8 << 20, pairs),
        )(doc_lengths, q_rot, d_out, third, lse_in, *blocks[1:], *dq_in)

    def plus(*xs):
        return functools.reduce(jnp.add, [x.astype(F32) for x in xs]).astype(BF16)

    lse_b = after(lse, *sends)
    if paired:
        dq_far, (d4, d3), delta = backward_far(0, 2, lse_b, attn, [])
        r3 = shift(d3, swap)
        dq_far, (d2, d1) = backward_far(2, 4, lse_b, delta, [dq_far])
        none = jnp.zeros_like(r3)
        sum4 = plus(d4, jnp.where(odd, r3, none))
        b2 = shift(sum4, hop_back)
        r1 = shift(d1, swap)
    else:
        dq_far, far, delta = backward_far(0, back, lse_b, attn, [])

    seconds = [firsts[1], firsts[0]]
    extra = [a for a in lead if a[0] == "dp" and a not in firsts]
    sends = []
    for c in range(2):
        color[c].addends[-1] = after(color[c].addends[-1], dq_far)
        for axis in [seconds[c]] + extra:
            sends.append(color[c].pick(axis, 1))
            color[c] = color[c].step(axis, move(sends[-1], axis))

    dq_near = after(dq_far, *sends)
    near_kb = max(kb // 2, 8)
    q_grad, own = pl.pallas_call(
        functools.partial(near_kernel, near_kb),
        grid=(tok // qb,),
        out_shape=(sds((tok, width), BF16), sds((tok, 2 * HEAD), F32)),
        in_specs=[SMEM_SPEC, tok_spec, tok_spec, lse_spec, lse_spec, dq_spec, VMEM_SPEC, table_spec, table_spec],
        out_specs=(tok_spec, pl.BlockSpec((tok, 2 * HEAD), lambda i: (0, 0))),
        scratch_shapes=[pltpu.VMEM((tok, HEAD), F32), pltpu.VMEM((tok, HEAD), F32)],
        compiler_params=params(NEAR_MIB, "arbitrary"),
        cost_estimate=cost(8 * heads * tok * tok * HEAD, 4 << 20, heads * tok * tok),
        name="near",
    )(doc_lengths, q_rot, d_out, delta, lse, dq_near, kv_home, cos, sin)

    ctx_axes = [("ctx", 0)] + [("ctx", b) for b in range(2, bits_ctx)]
    lse_bits = [1, 0] + list(range(2, bits_ctx))
    both = None
    for axis in ctx_axes:
        if both is None:
            pieces = [jnp.concatenate([color[c].pick(axis, w) for c in range(2)], axis=-2) for w in range(2)]
            left = [a for a in color[0].left if a != axis]
            send = after(pieces[1], own)
            kept = [pieces[0]]
        else:
            send = both.pick(axis, 1)
            left = [a for a in both.left if a != axis]
            at = both.left.index(axis)
            kept = [lax.index_in_dim(x, 0, at, keepdims=False) for x in both.addends]
        size = send.size // col
        recv = move(with_lse(send, lines), axis)
        if axis != ctx_axes[-1]:
            both = Parts(kept + [recv[:size].reshape(send.shape)], left)
            lines = jnp.concatenate([lines, recv[size:]], axis=0)
    last = functools.reduce(jnp.add, [x.astype(F32) for x in kept]).astype(BF16)

    if paired:
        sum2 = plus(d2, b2, jnp.where(odd, r1, r3))
        arrived = [shift(after(sum2, own), hop_back), jnp.where(odd, none, r1)]
    else:
        arrived = [
            shift(far[back - s], [(i + s, i) for i in range(n_ctx - s)]) for s in range(1, back + 1)
        ]
    k_grad, v_grad = pl.pallas_call(
        functools.partial(home_kernel, len(arrived)),
        out_shape=(sds((tok, HEAD), BF16), sds((tok, HEAD), BF16)),
        in_specs=[VMEM_SPEC] * (3 + len(arrived)),
        out_specs=(VMEM_SPEC, VMEM_SPEC),
        compiler_params=params(4),
        cost_estimate=cost(1 << 20, 2 << 20),
        name="home",
    )(own, cos, sin, *arrived)

    if col != HEAD:
        tail_rows = recv[width:].reshape(-1, HEAD)
        recv = jnp.concatenate([jnp.pad(recv[:width], ((0, 0), (0, HEAD - col))), tail_rows], axis=0)
        last = jnp.pad(last, ((0, 0), (0, HEAD - col)))
        lines = lines.reshape(-1, HEAD)
    wgrad, owner_lse = pl.pallas_call(
        functools.partial(final_kernel, lse_bits),
        out_shape=(sds((width, HEAD), F32), sds((heads, tok), F32)),
        in_specs=[SMEM_SPEC] + [VMEM_SPEC] * 3,
        out_specs=(VMEM_SPEC,) * 2,
        scratch_shapes=[pltpu.VMEM((2 * lines.size // HEAD, HEAD), F32)],
        compiler_params=params(8),
        cost_estimate=cost(1 << 18, 1 << 20),
        name="final",
    )(owner[0], last, recv, lines)
    wgrad = wgrad[:, :col]
    owner_lse = jnp.transpose(owner_lse)

    return (attn_out[None], q_grad[None], k_grad[None], v_grad[None], wgrad, owner_lse[None, None])


def solution(mesh):
    in_specs = (
        P("dp", "ctx", None),
        P("dp", "ctx", None),
        P("dp", "ctx", None),
        P("dp", None),
        P("dp", None),
        P(),
        P("dp", "ctx", None),
    )
    out_specs = (
        P("dp", "ctx", None),
        P("dp", "ctx", None),
        P("dp", "ctx", None),
        P("dp", "ctx", None),
        P(None, ("dp", "ctx")),
        P("dp", "ctx", None, None),
    )

    return jax.shard_map(on_device, mesh=mesh, in_specs=in_specs, out_specs=out_specs, check_vma=False)
```
